128 devices in a mesh: grp: 4 (over z), dev: 32 (over y, x, core).
Axes of the slice: x: 4, y: 4, z: 4, core: 2. Of those that a mesh axis runs over, the one named last changes fastest.
Arguments:
- coef: bfloat16 [2048, 393216], P('dev', 'grp'), may hold values from -6 to 6
- basis_idx: int32 [64, 512], replicated, may hold values from 0 to 255
- basis_w: float32 [64, 8, 512], replicated, may hold values from -0.25 to 0.25
- owner_blocks: int32 [256], replicated, may hold values from 0 to 255, each once
- data: float32 [393216], P(('grp', 'dev')), may hold values from -6 to 6
- panel_live: int32 [128], P(('grp', 'dev')), may hold values from 2304 to 3072, as said below
Outputs:
- r_factor: float32 [512, 512], replicated
- projected: float32 [512], replicated
- q_rows: float32 [393216, 512], P(('grp', 'dev'))
The draws below stay inside these ranges and needn't reach their ends.
Inputs may be any that keep to these rules, and one draw needn't show every extreme that they name: `owner_blocks`: each block index appears once. `panel_live`: some panel is full in every draw.
All inputs are finite; a program needn't handle non-finite values.
Results may differ from the reference program's by a relative error of at most 0.0038.
Values may be sent and summed in bfloat16 or wider, within the bound.
A program may use at most 128 MiB of HBM per device.

```python
import jax
import jax.numpy as jnp
from jax import lax

K = 512
NBLK = 256
BW = 8
NB_PER = 64
ROWS_DEV = 3072
NCOEF = 2048
PANELS = 128
ROWS = 393216


def draw_panel_live(key, part):
    counts_drawn = jax.random.randint(key, (PANELS,), 3 * ROWS_DEV // 4, ROWS_DEV + 1)
    full_spot = jax.random.randint(jax.random.fold_in(key, 7), (), 0, PANELS)
    least_spot = (full_spot + 1 + jax.random.randint(jax.random.fold_in(key, 11), (), 0, PANELS - 1)) % PANELS
    counts_drawn = counts_drawn.at[least_spot].set(3 * ROWS_DEV // 4)
    counts_drawn = counts_drawn.at[full_spot].set(ROWS_DEV)
    return counts_drawn.astype(jnp.int32)


def with_ends(array, own_key, smallest, top_value):
    longest = array.shape.index(max(array.shape))
    spots = []
    for shift in (0, 1):
        where = [jax.random.randint(jax.random.fold_in(own_key, axis), (), 0, length) for axis, length in enumerate(array.shape)]
        where[longest] = (where[longest] + shift) % array.shape[longest]
        spots.append(tuple(where))
    return array.at[spots[0]].set(smallest).at[spots[1]].set(top_value)


def level_of(own_key, shape, shards, low, high):
    def one(dim, blocks):
        draws = jax.random.uniform(jax.random.fold_in(jax.random.fold_in(own_key, 6), dim), (blocks,), jnp.float32, low / len(shards), high / len(shards))
        return jnp.repeat(jnp.exp(draws), shape[dim] // blocks).reshape((-1,) + (1,) * (len(shape) - dim - 1))

    factor_of = one(*shards[0])
    for cut in shards[1:]:
        factor_of = factor_of * one(*cut)
    return factor_of


def scatter_about(stream_key, dims, width, reach, pieces=(), kind=jnp.bfloat16):
    array = width * jax.random.normal(stream_key, dims, jnp.float32)
    if pieces:
        array = array * level_of(stream_key, dims, pieces, -0.22, 0.18)
    return jnp.clip(array, -reach, reach).astype(kind)


def setup_inputs(seed: int = 0) -> dict:
    key_list = jax.random.split(jax.random.key(seed), 7)
    coef = scatter_about(key_list[0], (NCOEF, ROWS), 1.0, 6.0, ((0, 32), (1, 4)))
    basis_idx = with_ends(jax.random.randint(key_list[1], (NB_PER, K), 0, NBLK), jax.random.fold_in(key_list[1], 1), 0, NBLK - 1).astype(jnp.int32)
    basis_w = scatter_about(key_list[2], (NB_PER, BW, K), (NB_PER * BW) ** -0.5, 0.25, (), jnp.float32)
    owner_blocks = jax.random.permutation(key_list[3], NBLK).astype(jnp.int32)
    data = scatter_about(key_list[4], (ROWS,), 1.0, 6.0, ((0, 128),), jnp.float32)
    panel_live = draw_panel_live(jax.random.fold_in(key_list[6], 71), 0)
    return {"coef": coef, "basis_idx": basis_idx, "basis_w": basis_w, "owner_blocks": owner_blocks, "data": data, "panel_live": panel_live}


def build_basis(basis_idx, basis_w, owner_blocks):
    one_hot = (basis_idx[:, None, :] == owner_blocks[None, :, None]).astype(jnp.float32)
    dense_basis = jnp.einsum('tbk,tdk->bdk', one_hot, basis_w.astype(jnp.float32), precision=lax.Precision.HIGHEST)
    return dense_basis.reshape(-1, dense_basis.shape[2]).astype(jnp.bfloat16)

def panel_green(coef, dense_basis, panel_id, live_rows):
    row_index = jnp.arange(ROWS_DEV, dtype=jnp.int32)
    offset = (panel_id * ROWS_DEV).astype(jnp.int32)
    block_coef = lax.dynamic_slice_in_dim(coef, offset, ROWS_DEV, 1)
    row_mask = row_index < live_rows
    green_rows = lax.dot_general(block_coef.astype(jnp.float32), dense_basis.astype(jnp.float32), (((0,), (0,)), ((), ())), preferred_element_type=jnp.float32)
    return (jnp.where(row_mask[:, None], green_rows, jnp.float32(0.0)), row_mask)

def reference(coef, basis_idx, basis_w, owner_blocks, data, panel_live):
    dense_basis = build_basis(basis_idx, basis_w, owner_blocks)
    panel_data = data.reshape(PANELS, ROWS_DEV)
    panel_ids = jnp.arange(PANELS, dtype=jnp.int32)

    def add_panel(carry, items):
        gram_sum, rhs_sum = carry
        panel_id, block_data, live_rows = items
        green_rows, row_mask = panel_green(coef, dense_basis, panel_id, live_rows)
        live_data = jnp.where(row_mask, block_data, jnp.float32(0.0))
        gram_sum = gram_sum + jnp.dot(green_rows.T, green_rows, precision=lax.Precision.HIGHEST)
        rhs_sum = rhs_sum + jnp.dot(live_data, green_rows, precision=lax.Precision.HIGHEST)
        return ((gram_sum, rhs_sum), None)
    start = (jnp.zeros((K, K), jnp.float32), jnp.zeros((K,), jnp.float32))
    (gram_sum, rhs_sum), _ = lax.scan(add_panel, start, (panel_ids, panel_data, panel_live))
    lower = jnp.linalg.cholesky(gram_sum)
    projected = jax.scipy.linalg.solve_triangular(lower, rhs_sum, lower=True)
    r_factor = lower.T / jnp.sqrt(jnp.float32(ROWS))

    def panel_q(items):
        panel_id, live_rows = items
        green_rows, row_mask = panel_green(coef, dense_basis, panel_id, live_rows)
        return jax.scipy.linalg.solve_triangular(r_factor.T, green_rows.T, lower=True).T
    q_rows = lax.map(panel_q, (panel_ids, panel_live)).reshape(ROWS, K)
    return (r_factor, projected, q_rows)
```

```python
import functools

import jax
import jax.numpy as jnp
from jax import lax
from jax.experimental import pallas as pl
from jax.experimental.pallas import tpu as pltpu
from jax.sharding import PartitionSpec as P

HI = lax.Precision.HIGHEST
MESH = pl.DeviceIdType.MESH
NB = 128
SB = 8
CHUNK = 256
BLK = 8
NY, NX, NC, NZ = 4, 4, 2, 4
NCHIP = NY * NX
NDEV = NCHIP * NC
PIECE = 48
HALF = NCHIP * PIECE


def hops(oy, ox):
    return min(oy, NY - oy) + min(ox, NX - ox)


def peer_offsets():
    offs = [(oy, ox, oc) for oy in range(NY) for ox in range(NX) for oc in range(NC)]
    return sorted(offs[1:], key=lambda o: hops(o[0], o[1]))


def chip_offsets():
    offs = [(oy, ox) for oy in range(NY) for ox in range(NX)][1:]
    return sorted(offs, key=lambda o: -hops(o[0], o[1]))


def upper_blocks(k):
    n = k // NB
    return [(p, q) for p in range(n) for q in range(p, n)]


def dot_t(a, b):
    return lax.dot_general(a, b, (((0,), (0,)), ((), ())), preferred_element_type=jnp.float32)


def split(x):
    high = x.astype(jnp.bfloat16)
    return high, (x - high.astype(jnp.float32)).astype(jnp.bfloat16)


def green_kernel(
    owner_ref, live_ref, coef_ref, idx_ref, w_ref, data_ref,
    green_ref, sum_ref,
    panel, basis, gbuf, gram, rhs, packed, half, from_core, from_chip, from_z, total,
    send_a, recv_a, local_a, out_g, send_c, recv_c, send_p, recv_p, send_z, recv_z, send_g, recv_g, send_f, recv_f,
):
    rows = green_ref.shape[0]
    k = green_ref.shape[1]
    depth = coef_ref.shape[0]
    chunks = rows // CHUNK
    z, me = lax.axis_index("grp"), lax.axis_index("dev")
    c, x, y = me % NC, (me // NC) % NX, me // (NC * NX)
    chip = y * NX + x
    partner = chip * NC + (1 - c)
    peers = peer_offsets()
    chips = chip_offsets()

    def device_at(oy, ox, oc):
        return (lax.rem(y + oy, NY) * NX + lax.rem(x + ox, NX)) * NC + lax.rem(c + oc, NC)

    barrier = pltpu.get_barrier_semaphore()
    for off in peers:
        pl.semaphore_signal(barrier, inc=1, device_id=(z, device_at(*off)), device_id_type=MESH)
    for oz in range(1, NZ):
        pl.semaphore_signal(barrier, inc=1, device_id=(lax.rem(z + oz, NZ), me), device_id_type=MESH)
    pl.semaphore_wait(barrier, len(peers) + NZ - 1)

    def coef_copy(ch, i):
        to = device_at(*peers[i])
        at = pl.ds(pl.multiple_of(to * rows + ch * CHUNK, NB), CHUNK)
        return pltpu.make_async_remote_copy(
            src_ref=coef_ref.at[:, at], dst_ref=panel.at[ch, me],
            send_sem=send_a.at[ch, i], recv_sem=recv_a.at[ch, i],
            device_id=(z, to), device_id_type=MESH,
        )

    def own_copy(ch):
        at = pl.ds(pl.multiple_of(me * rows + ch * CHUNK, NB), CHUNK)
        return pltpu.make_async_copy(coef_ref.at[:, at], panel.at[ch, me], local_a.at[ch])

    def start_chunk(ch, carry):
        own_copy(ch).start()
        for i in range(len(peers)):
            coef_copy(ch, i).start()
        return carry

    lax.fori_loop(0, chunks, start_chunk, 0)

    group = 4
    slots = idx_ref.shape[0]

    def build(step, carry):
        parts = [jnp.zeros((BLK, k), jnp.float32) for _ in range(group)]
        owners = [owner_ref[step * group + i] for i in range(group)]
        for t in range(slots):
            ids = jnp.broadcast_to(idx_ref[t:t + 1, :], (BLK, k))
            weights = w_ref[t]
            for i in range(group):
                parts[i] = parts[i] + jnp.where(ids == owners[i], weights, 0.0)
        at = pl.ds(pl.multiple_of(step * group * BLK, group * BLK), group * BLK)
        basis[at, :] = jnp.concatenate(parts, axis=0).astype(jnp.bfloat16)
        return carry

    lax.fori_loop(0, basis.shape[0] // (group * BLK), build, 0)

    gram[...] = jnp.zeros_like(gram)
    rhs[...] = jnp.zeros_like(rhs)

    def green_out(ch):
        at = pl.ds(pl.multiple_of(ch * CHUNK, CHUNK), CHUNK)
        return pltpu.make_async_copy(gbuf.at[at, :], green_ref.at[at, :], out_g.at[ch])

    def work_chunk(ch, carry):
        own_copy(ch).wait()
        for i in range(len(peers)):
            coef_copy(ch, i).wait_recv()
        block = panel[ch].reshape(NDEV * depth, CHUNK)
        green = dot_t(block, basis[...])
        row = lax.broadcasted_iota(jnp.int32, (CHUNK, k), 0) + ch * CHUNK
        green = jnp.where(row < live_ref[0], green, 0.0)
        at = pl.ds(pl.multiple_of(ch * CHUNK, CHUNK), CHUNK)
        gbuf[at, :] = green
        green_out(ch).start()
        high, low = split(green)
        gram[...] += dot_t(high, high) + (dot_t(high, low) + dot_t(low, high))
        line = jnp.broadcast_to(data_ref[:, at], (SB, CHUNK))
        column = jnp.transpose(line)[:, :1]
        rhs[...] += jnp.sum((green * column).reshape(CHUNK // SB, SB, k), axis=0)
        return carry

    lax.fori_loop(0, chunks, work_chunk, 0)

    blocks = upper_blocks(k)
    for i, (p, q) in enumerate(blocks):
        packed[i * NB:(i + 1) * NB, :] = gram[p * NB:(p + 1) * NB, q * NB:(q + 1) * NB]
    used = len(blocks) * NB
    packed[used:, :] = jnp.zeros((2 * HALF - used, NB), jnp.float32)
    rhs_row = jnp.sum(rhs[...], axis=0, keepdims=True)
    for i in range(k // NB):
        packed[used + i:used + i + 1, :] = rhs_row[:, i * NB:(i + 1) * NB]

    mine = pl.ds(pl.multiple_of(c * HALF, HALF), HALF)
    other = pl.ds(pl.multiple_of((1 - c) * HALF, HALF), HALF)
    core_copy = pltpu.make_async_remote_copy(
        src_ref=packed.at[other, :], dst_ref=from_core, send_sem=send_c, recv_sem=recv_c,
        device_id=(z, partner), device_id_type=MESH,
    )
    core_copy.start()
    core_copy.wait_recv()
    half[...] = packed[mine, :] + from_core[...]

    def chip_at(oy, ox):
        return lax.rem(y + oy, NY) * NX + lax.rem(x + ox, NX)

    def piece_copy(i):
        to = chip_at(*chips[i])
        return pltpu.make_async_remote_copy(
            src_ref=half.at[pl.ds(pl.multiple_of(to * PIECE, SB), PIECE), :], dst_ref=from_chip.at[i],
            send_sem=send_p.at[i], recv_sem=recv_p.at[i],
            device_id=(z, to * NC + c), device_id_type=MESH,
        )

    for i in range(len(chips)):
        piece_copy(i).start()
    part = half[pl.ds(pl.multiple_of(chip * PIECE, SB), PIECE), :]
    for i in reversed(range(len(chips))):
        piece_copy(i).wait_recv()
        part = part + from_chip[i]
    from_z[z] = part

    def z_copy(oz):
        return pltpu.make_async_remote_copy(
            src_ref=from_z.at[z], dst_ref=from_z.at[z], send_sem=send_z.at[oz - 1], recv_sem=recv_z.at[oz - 1],
            device_id=(lax.rem(z + oz, NZ), me), device_id_type=MESH,
        )

    for oz in (2, 1, 3):
        z_copy(oz).start()
    for oz in (1, 3, 2):
        z_copy(oz).wait_recv()

    def piece_of(chip_id):
        return pl.ds(pl.multiple_of(c * HALF + chip_id * PIECE, SB), PIECE)

    total[piece_of(chip), :] = (from_z[0] + from_z[1]) + (from_z[2] + from_z[3])

    def gather_copy(i):
        to = chip_at(*chips[i])
        return pltpu.make_async_remote_copy(
            src_ref=total.at[piece_of(chip), :], dst_ref=total.at[piece_of(chip), :],
            send_sem=send_g.at[i], recv_sem=recv_g.at[i],
            device_id=(z, to * NC + c), device_id_type=MESH,
        )

    def pass_on(chip_id, i):
        return pltpu.make_async_remote_copy(
            src_ref=total.at[piece_of(chip_id), :], dst_ref=total.at[piece_of(chip_id), :],
            send_sem=send_f.at[i], recv_sem=recv_f.at[i],
            device_id=(z, partner), device_id_type=MESH,
        )

    last = len(chips)
    for i in range(last):
        gather_copy(i).start()
    pass_on(chip, last).start()
    for i in reversed(range(last)):
        oy, ox = chips[i]
        gather_copy(i).wait_recv()
        pass_on(chip_at(NY - oy, NX - ox), i).start()
    for i in range(last + 1):
        pass_on(chip, i).wait()
    sum_ref[...] = total[...]

    core_copy.wait_send()
    for i in range(last):
        piece_copy(i).wait_send()
        gather_copy(i).wait_send()
    for oz in range(1, NZ):
        z_copy(oz).wait_send()

    def finish(ch, carry):
        green_out(ch).wait()
        for i in range(len(peers)):
            coef_copy(ch, i).wait_send()
        return carry

    lax.fori_loop(0, chunks, finish, 0)


def green_call(coef, basis_idx, basis_w, owner_blocks, data, panel_live):
    depth = coef.shape[0]
    rows = data.shape[0]
    k = basis_idx.shape[1]
    chunks = rows // CHUNK
    peers, chips = NDEV - 1, NCHIP - 1
    vmem = pl.BlockSpec(memory_space=pltpu.VMEM)
    smem = pl.BlockSpec(memory_space=pltpu.SMEM)
    anywhere = pl.BlockSpec(memory_space=pl.ANY)
    dma = pltpu.SemaphoreType.DMA
    f32 = jnp.float32
    return pl.pallas_call(
        green_kernel,
        out_shape=(jax.ShapeDtypeStruct((rows, k), f32), jax.ShapeDtypeStruct((2 * HALF, NB), f32)),
        in_specs=[smem, smem, anywhere, vmem, vmem, vmem],
        out_specs=(anywhere, vmem),
        scratch_shapes=[
            pltpu.VMEM((chunks, NDEV, depth, CHUNK), jnp.bfloat16),
            pltpu.VMEM((NDEV * depth, k), jnp.bfloat16),
            pltpu.VMEM((rows, k), f32),
            pltpu.VMEM((k, k), f32),
            pltpu.VMEM((SB, k), f32),
            pltpu.VMEM((2 * HALF, NB), f32),
            pltpu.VMEM((HALF, NB), f32),
            pltpu.VMEM((HALF, NB), f32),
            pltpu.VMEM((chips, PIECE, NB), f32),
            pltpu.VMEM((NZ, PIECE, NB), f32),
            pltpu.VMEM((2 * HALF, NB), f32),
            dma((chunks, peers)), dma((chunks, peers)), dma((chunks,)), dma((chunks,)),
            dma, dma, dma((chips,)), dma((chips,)), dma((NZ - 1,)), dma((NZ - 1,)),
            dma((chips,)), dma((chips,)), dma((chips + 1,)), dma((chips + 1,)),
        ],
        name="green",
        compiler_params=pltpu.CompilerParams(collective_id=0, has_side_effects=True, vmem_limit_bytes=56 << 20),
    )(owner_blocks, panel_live, coef, basis_idx, basis_w, data.reshape(1, rows))


def dot_hi(a, b, ca, cb):
    return lax.dot_general(a, b, (((ca,), (cb,)), ((), ())), precision=HI, preferred_element_type=jnp.float32)


def factor_block(d, v):
    n = len(d)
    sub = lax.broadcasted_iota(jnp.int32, (SB, NB), 0)

    def spread(part):
        return jnp.broadcast_to(part, (SB, NB))

    for g in range(n):
        j0 = SB * g
        cols = [spread(d[g][:, j0 + c:j0 + c + 1]) for c in range(SB)]
        invs, pd, pv, cross = [], [], [], []
        for c in range(SB):
            row = [None] * SB
            invs.append(1.0 / spread(cols[c][c:c + 1, :]))
            pd.append(spread(d[g][c:c + 1, :]))
            pv.append(spread(v[g][c:c + 1, :]))
            m = jnp.where(sub > c, cols[c] * invs[c], 0.0)
            for c2 in range(c + 1, SB):
                row[c2] = spread(cols[c2][c:c + 1, :])
                cols[c2] = cols[c2] - m * row[c2]
            cross.append(row)
            d[g] = d[g] - m * pd[c]
            v[g] = v[g] - m * pv[c]
        for i in range(g + 1, n):
            cols = [spread(d[i][:, j0 + c:j0 + c + 1]) for c in range(SB)]
            for c in range(SB):
                m = cols[c] * invs[c]
                for c2 in range(c + 1, SB):
                    cols[c2] = cols[c2] - m * cross[c][c2]
                d[i] = d[i] - m * pd[c]
                v[i] = v[i] - m * pv[c]
    return d, v


def factor_kernel(rows_total, tile, sum_ref, green_ref, r_ref, z_ref, q_ref, a, w, gbuf, qbuf, gsem, qsem):
    k = r_ref.shape[0]
    rows = green_ref.shape[0]
    nblk = k // NB
    get = pltpu.make_async_copy(green_ref, gbuf, gsem)
    get.start()
    a[...] = jnp.zeros_like(a)
    w[...] = jnp.zeros_like(w)
    blocks = upper_blocks(k)
    for i, (p, q) in enumerate(blocks):
        a[p * NB:(p + 1) * NB, q * NB:(q + 1) * NB] = sum_ref[i * NB:(i + 1) * NB, :]
    used = len(blocks) * NB
    rhs = jnp.concatenate([sum_ref[used + i:used + i + 1, :] for i in range(nblk)], axis=1)
    ri = lax.broadcasted_iota(jnp.int32, (NB, NB), 0)
    ci = lax.broadcasted_iota(jnp.int32, (NB, NB), 1)
    eye = jnp.where(ri == ci, 1.0, 0.0)
    for p in range(nblk):
        w[p * NB:(p + 1) * NB, p * NB:(p + 1) * NB] = eye

    def panel(p, carry):
        first = pl.multiple_of(p * NB, NB)
        at = pl.ds(first, NB)
        d = [a[pl.ds(first + SB * i, SB), at] for i in range(NB // SB)]
        v = [eye[SB * i:SB * i + SB] for i in range(NB // SB)]
        d, v = factor_block(d, v)
        dd = jnp.concatenate(d, axis=0)
        scale = lax.rsqrt(jnp.sum(jnp.where(ri == ci, dd, 0.0), axis=1, keepdims=True))
        vv = jnp.where(ri >= ci, jnp.concatenate(v, axis=0) * scale, 0.0)
        urow = dot_hi(vv, a[at, :], 1, 0)
        lane = lax.broadcasted_iota(jnp.int32, (NB, k), 1)
        urow = jnp.where(lane >= first + NB, urow, 0.0)
        a[at, :] = urow
        a[at, at] = jnp.where(ri <= ci, dd * scale, 0.0)
        wrow = dot_hi(vv, w[at, :], 1, 0)
        w[at, :] = wrow
        for q in range(1, nblk):
            @pl.when(q > p)
            def _():
                qs = slice(q * NB, (q + 1) * NB)
                u = a[at, qs]
                a[qs, :] = a[qs, :] - dot_hi(u, urow, 0, 0)
                w[qs, :] = w[qs, :] - dot_hi(u, wrow, 0, 0)
        return carry

    lax.fori_loop(0, nblk, panel, 0)
    for p in range(1, nblk):
        a[p * NB:(p + 1) * NB, :p * NB] = jnp.zeros((NB, p * NB), jnp.float32)
    r_ref[...] = a[...] * (1.0 / rows_total ** 0.5)
    z_ref[...] = dot_hi(rhs, w[...], 1, 1)
    inv_high, inv_low = split(w[...] * (rows_total ** 0.5))
    get.wait()

    def q_out(t):
        at = slice(t * tile, (t + 1) * tile)
        return pltpu.make_async_copy(qbuf.at[at, :], q_ref.at[at, :], qsem.at[t])

    def dot_n(left, right):
        return lax.dot_general(left, right, (((1,), (1,)), ((), ())), preferred_element_type=jnp.float32)

    for t in range(rows // tile):
        at = slice(t * tile, (t + 1) * tile)
        high, low = split(gbuf[at, :])
        qbuf[at, :] = dot_n(high, inv_high) + (dot_n(low, inv_high) + dot_n(high, inv_low))
        q_out(t).start()
    for t in range(rows // tile):
        q_out(t).wait()


def factor_call(gram_sum, green, rows_total):
    rows, k = green.shape
    tile = 512
    vmem = pl.BlockSpec(memory_space=pltpu.VMEM)
    anywhere = pl.BlockSpec(memory_space=pl.ANY)
    f32 = jnp.float32
    return pl.pallas_call(
        functools.partial(factor_kernel, rows_total, tile),
        out_shape=(jax.ShapeDtypeStruct((k, k), f32), jax.ShapeDtypeStruct((1, k), f32), jax.ShapeDtypeStruct((rows, k), f32)),
        in_specs=[vmem, anywhere],
        out_specs=(vmem, vmem, anywhere),
        scratch_shapes=[
            pltpu.VMEM((k, k), f32), pltpu.VMEM((k, k), f32),
            pltpu.VMEM((rows, k), f32), pltpu.VMEM((rows, k), f32),
            pltpu.SemaphoreType.DMA, pltpu.SemaphoreType.DMA((rows // tile,)),
        ],
        name="factor",
        compiler_params=pltpu.CompilerParams(vmem_limit_bytes=40 << 20),
    )(gram_sum, green)


def on_device(coef, basis_idx, basis_w, owner_blocks, data, panel_live):
    green, gram_sum = green_call(coef, basis_idx, basis_w, owner_blocks, data, panel_live)
    rows_total = green.shape[0] * lax.axis_size("dev") * lax.axis_size("grp")
    r_factor, projected, q_rows = factor_call(gram_sum, green, rows_total)
    return (r_factor, projected.reshape(-1), q_rows)


def solution(mesh):
    in_specs = (P("dev", "grp"), P(), P(), P(), P(("grp", "dev")), P(("grp", "dev")))
    out_specs = (P(), P(), P(("grp", "dev"), None))
    return jax.shard_map(
        on_device, mesh=mesh, in_specs=in_specs, out_specs=out_specs, check_vma=False
    )
```

```python
import functools

import jax
import jax.numpy as jnp
from jax import lax
from jax.experimental import pallas as pl
from jax.experimental.pallas import tpu as pltpu
from jax.sharding import PartitionSpec as P

HI = lax.Precision.HIGHEST
MESH = pl.DeviceIdType.MESH
NB = 128
SB = 8
CHUNK = 256
BLK = 8
NY, NX, NC, NZ = 4, 4, 2, 4
NCHIP = NY * NX
NDEV = NCHIP * NC
PIECE = 40
HALF = NCHIP * PIECE
RHS_AT = 120
RHS_W = 64


def hops(oy, ox):
    return min(oy, NY - oy) + min(ox, NX - ox)


def peer_offsets():
    offs = [(oy, ox, oc) for oy in range(NY) for ox in range(NX) for oc in range(NC)]
    return sorted(offs[1:], key=lambda o: hops(o[0], o[1]))


def chip_offsets():
    offs = [(oy, ox) for oy in range(NY) for ox in range(NX)][1:]
    return sorted(offs, key=lambda o: -hops(o[0], o[1]))


def upper_blocks(k):
    n = k // NB
    return [(p, q) for p in range(n) for q in range(p, n)]


def dot_t(a, b):
    return lax.dot_general(a, b, (((0,), (0,)), ((), ())), preferred_element_type=jnp.float32)


def split(x):
    high = x.astype(jnp.bfloat16)
    return high, (x - high.astype(jnp.float32)).astype(jnp.bfloat16)


def green_kernel(
    owner_ref, live_ref, coef_ref, idx_hbm, w_hbm, data_ref,
    green_ref, sum_ref,
    panel, basis, gbuf, idx_ref, w_ref, rhs, packed, half, from_core, from_chip, from_z, total, load,
    send_a, recv_a, local_a, out_g, send_c, recv_c, send_p, recv_p, send_z, recv_z, send_g, recv_g, send_f, recv_f,
):
    rows = green_ref.shape[0]
    k = green_ref.shape[1]
    depth = coef_ref.shape[0]
    chunks = rows // CHUNK
    z, me = lax.axis_index("grp"), lax.axis_index("dev")
    c, x, y = me % NC, (me // NC) % NX, me // (NC * NX)
    chip = y * NX + x
    partner = chip * NC + (1 - c)
    peers = peer_offsets()
    chips = chip_offsets()

    def device_at(oy, ox, oc):
        return (lax.rem(y + oy, NY) * NX + lax.rem(x + ox, NX)) * NC + lax.rem(c + oc, NC)

    loads = [pltpu.make_async_copy(idx_hbm, idx_ref, load.at[0]), pltpu.make_async_copy(w_hbm, w_ref, load.at[1])]
    for one in loads:
        one.start()

    barrier = pltpu.get_barrier_semaphore()
    for off in peers:
        pl.semaphore_signal(barrier, inc=1, device_id=(z, device_at(*off)), device_id_type=MESH)
    for oz in range(1, NZ):
        pl.semaphore_signal(barrier, inc=1, device_id=(lax.rem(z + oz, NZ), me), device_id_type=MESH)
    pl.semaphore_wait(barrier, len(peers) + NZ - 1)

    def coef_copy(ch, i):
        to = device_at(*peers[i])
        at = pl.ds(pl.multiple_of(to * rows + ch * CHUNK, NB), CHUNK)
        return pltpu.make_async_remote_copy(
            src_ref=coef_ref.at[:, at], dst_ref=panel.at[ch, me],
            send_sem=send_a.at[ch, i], recv_sem=recv_a.at[ch, i],
            device_id=(z, to), device_id_type=MESH,
        )

    def own_copy(ch):
        at = pl.ds(pl.multiple_of(me * rows + ch * CHUNK, NB), CHUNK)
        return pltpu.make_async_copy(coef_ref.at[:, at], panel.at[ch, me], local_a.at[ch])

    def start_chunk(ch, carry):
        own_copy(ch).start()
        for i in range(len(peers)):
            coef_copy(ch, i).start()
        return carry

    lax.fori_loop(0, chunks, start_chunk, 0)

    group = 4
    slots = idx_ref.shape[0]

    def build(step, carry):
        parts = [jnp.zeros((BLK, k), jnp.float32) for _ in range(group)]
        owners = [owner_ref[step * group + i] for i in range(group)]
        for t in range(slots):
            ids = jnp.broadcast_to(idx_ref[t:t + 1, :], (BLK, k))
            weights = w_ref[t]
            for i in range(group):
                parts[i] = parts[i] + jnp.where(ids == owners[i], weights, 0.0)
        at = pl.ds(pl.multiple_of(step * group * BLK, group * BLK), group * BLK)
        basis[at, :] = jnp.concatenate(parts, axis=0).astype(jnp.bfloat16)
        return carry

    for one in loads:
        one.wait()
    lax.fori_loop(0, basis.shape[0] // (group * BLK), build, 0)

    blocks = upper_blocks(k)
    packed[...] = jnp.zeros_like(packed)
    rhs[...] = jnp.zeros_like(rhs)

    def green_out(ch):
        at = pl.ds(pl.multiple_of(ch * CHUNK, CHUNK), CHUNK)
        return pltpu.make_async_copy(gbuf.at[at, :], green_ref.at[at, :], out_g.at[ch])

    def work_chunk(ch, carry):
        own_copy(ch).wait()
        for i in range(len(peers)):
            coef_copy(ch, i).wait_recv()

        @pl.when(ch > 0)
        def _():
            for i in range(len(peers)):
                coef_copy(ch - 1, i).wait_send()

        block = panel[ch].reshape(NDEV * depth, CHUNK)
        green = dot_t(block, basis[...])
        row = lax.broadcasted_iota(jnp.int32, (CHUNK, k), 0) + ch * CHUNK
        green = jnp.where(row < live_ref[0], green, 0.0)
        at = pl.ds(pl.multiple_of(ch * CHUNK, CHUNK), CHUNK)
        gbuf[at, :] = green
        green_out(ch).start()
        high, low = split(green)
        gram = dot_t(high, high) + (dot_t(high, low) + dot_t(low, high))
        for i, (p, q) in enumerate(blocks):
            packed[i * NB:(i + 1) * NB, :] += gram[p * NB:(p + 1) * NB, q * NB:(q + 1) * NB]
        line = jnp.broadcast_to(data_ref[:, at], (SB, CHUNK))
        column = jnp.transpose(line)[:, :1]
        rhs[...] += jnp.sum((green * column).reshape(CHUNK // SB, SB, k), axis=0)
        return carry

    lax.fori_loop(0, chunks, work_chunk, 0)

    rhs_row = jnp.sum(rhs[...], axis=0, keepdims=True)
    for i in range(k // RHS_W):
        packed[RHS_AT + i:RHS_AT + i + 1, :RHS_W] = rhs_row[:, i * RHS_W:(i + 1) * RHS_W]

    def chip_at(oy, ox):
        return lax.rem(y + oy, NY) * NX + lax.rem(x + ox, NX)

    band = NX * PIECE

    def core_copy(oy):
        at = lax.rem(y + oy, NY) * band
        return pltpu.make_async_remote_copy(
            src_ref=packed.at[pl.ds(pl.multiple_of((1 - c) * HALF + at, SB), band), :],
            dst_ref=from_core.at[pl.ds(pl.multiple_of(at, SB), band), :],
            send_sem=send_c.at[oy], recv_sem=recv_c.at[oy],
            device_id=(z, partner), device_id_type=MESH,
        )

    def piece_copy(i):
        to = chip_at(*chips[i])
        return pltpu.make_async_remote_copy(
            src_ref=half.at[pl.ds(pl.multiple_of(to * PIECE, SB), PIECE), :], dst_ref=from_chip.at[i],
            send_sem=send_p.at[i], recv_sem=recv_p.at[i],
            device_id=(z, to * NC + c), device_id_type=MESH,
        )

    bands = (2, 1, 3, 0)
    for oy in bands:
        core_copy(oy).start()
    for oy in bands:
        core_copy(oy).wait_recv()
        at = lax.rem(y + oy, NY) * band
        here = pl.ds(pl.multiple_of(at, SB), band)
        half[here, :] = packed[pl.ds(pl.multiple_of(c * HALF + at, SB), band), :] + from_core[here, :]
        for i in range(len(chips)):
            if chips[i][0] == oy:
                piece_copy(i).start()
    part = half[pl.ds(pl.multiple_of(chip * PIECE, SB), PIECE), :]
    for i in reversed(range(len(chips))):
        piece_copy(i).wait_recv()
        part = part + from_chip[i]
    from_z[z] = part

    def z_copy(oz):
        return pltpu.make_async_remote_copy(
            src_ref=from_z.at[z], dst_ref=from_z.at[z], send_sem=send_z.at[oz - 1], recv_sem=recv_z.at[oz - 1],
            device_id=(lax.rem(z + oz, NZ), me), device_id_type=MESH,
        )

    for oz in (2, 1, 3):
        z_copy(oz).start()
    for oz in (1, 3, 2):
        z_copy(oz).wait_recv()

    def piece_of(chip_id):
        return pl.ds(pl.multiple_of(c * HALF + chip_id * PIECE, SB), PIECE)

    total[piece_of(chip), :] = (from_z[0] + from_z[1]) + (from_z[2] + from_z[3])

    def gather_copy(i):
        to = chip_at(*chips[i])
        return pltpu.make_async_remote_copy(
            src_ref=total.at[piece_of(chip), :], dst_ref=total.at[piece_of(chip), :],
            send_sem=send_g.at[i], recv_sem=recv_g.at[i],
            device_id=(z, to * NC + c), device_id_type=MESH,
        )

    def pass_on(chip_id, i):
        return pltpu.make_async_remote_copy(
            src_ref=total.at[piece_of(chip_id), :], dst_ref=total.at[piece_of(chip_id), :],
            send_sem=send_f.at[i], recv_sem=recv_f.at[i],
            device_id=(z, partner), device_id_type=MESH,
        )

    last = len(chips)
    for i in range(last):
        gather_copy(i).start()
    pass_on(chip, last).start()
    for i in reversed(range(last)):
        oy, ox = chips[i]
        gather_copy(i).wait_recv()
        pass_on(chip_at(NY - oy, NX - ox), i).start()
    for i in range(last + 1):
        pass_on(chip, i).wait()
    sum_ref[...] = total[...]

    for oy in bands:
        core_copy(oy).wait_send()
    for i in range(last):
        piece_copy(i).wait_send()
        gather_copy(i).wait_send()
    for oz in range(1, NZ):
        z_copy(oz).wait_send()

    def finish(ch, carry):
        green_out(ch).wait()
        return carry

    lax.fori_loop(0, chunks, finish, 0)
    for i in range(len(peers)):
        coef_copy(chunks - 1, i).wait_send()


def green_call(coef, basis_idx, basis_w, owner_blocks, data, panel_live):
    depth = coef.shape[0]
    rows = data.shape[0]
    k = basis_idx.shape[1]
    chunks = rows // CHUNK
    peers, chips = NDEV - 1, NCHIP - 1
    vmem = pl.BlockSpec(memory_space=pltpu.VMEM)
    smem = pl.BlockSpec(memory_space=pltpu.SMEM)
    anywhere = pl.BlockSpec(memory_space=pl.ANY)
    dma = pltpu.SemaphoreType.DMA
    f32 = jnp.float32
    return pl.pallas_call(
        green_kernel,
        out_shape=(jax.ShapeDtypeStruct((rows, k), f32), jax.ShapeDtypeStruct((2 * HALF, NB), f32)),
        in_specs=[smem, smem, anywhere, anywhere, anywhere, vmem],
        out_specs=(anywhere, vmem),
        scratch_shapes=[
            pltpu.VMEM((chunks, NDEV, depth, CHUNK), jnp.bfloat16),
            pltpu.VMEM((NDEV * depth, k), jnp.bfloat16),
            pltpu.VMEM((rows, k), f32),
            pltpu.VMEM(basis_idx.shape, jnp.int32),
            pltpu.VMEM(basis_w.shape, f32),
            pltpu.VMEM((SB, k), f32),
            pltpu.VMEM((2 * HALF, NB), f32),
            pltpu.VMEM((HALF, NB), f32),
            pltpu.VMEM((HALF, NB), f32),
            pltpu.VMEM((chips, PIECE, NB), f32),
            pltpu.VMEM((NZ, PIECE, NB), f32),
            pltpu.VMEM((2 * HALF, NB), f32),
            dma((2,)), dma((chunks, peers)), dma((chunks, peers)), dma((chunks,)), dma((chunks,)),
            dma((NY,)), dma((NY,)), dma((chips,)), dma((chips,)), dma((NZ - 1,)), dma((NZ - 1,)),
            dma((chips,)), dma((chips,)), dma((chips + 1,)), dma((chips + 1,)),
        ],
        name="green",
        compiler_params=pltpu.CompilerParams(collective_id=0, has_side_effects=True, vmem_limit_bytes=56 << 20),
    )(owner_blocks, panel_live, coef, basis_idx, basis_w, data.reshape(1, rows))


def dot_hi(a, b, ca, cb):
    return lax.dot_general(a, b, (((ca,), (cb,)), ((), ())), precision=HI, preferred_element_type=jnp.float32)


def factor_block(d, v):
    n = len(d)
    sub = lax.broadcasted_iota(jnp.int32, (SB, NB), 0)

    def spread(part):
        return jnp.broadcast_to(part, (SB, NB))

    for g in range(n):
        j0 = SB * g
        cols = [spread(d[g][:, j0 + c:j0 + c + 1]) for c in range(SB)]
        invs, pd, pv, cross = [], [], [], []
        for c in range(SB):
            row = [None] * SB
            invs.append(1.0 / spread(cols[c][c:c + 1, :]))
            pd.append(spread(d[g][c:c + 1, :]))
            pv.append(spread(v[g][c:c + 1, :]))
            m = jnp.where(sub > c, cols[c] * invs[c], 0.0)
            for c2 in range(c + 1, SB):
                row[c2] = spread(cols[c2][c:c + 1, :])
                cols[c2] = cols[c2] - m * row[c2]
            cross.append(row)
            d[g] = d[g] - m * pd[c]
            v[g] = v[g] - m * pv[c]
        for i in range(g + 1, n):
            cols = [spread(d[i][:, j0 + c:j0 + c + 1]) for c in range(SB)]
            for c in range(SB):
                m = cols[c] * invs[c]
                for c2 in range(c + 1, SB):
                    cols[c2] = cols[c2] - m * cross[c][c2]
                d[i] = d[i] - m * pd[c]
                v[i] = v[i] - m * pv[c]
    return d, v


def factor_kernel(rows_total, tile, sum_ref, green_ref, r_ref, z_ref, q_ref, a, w, gbuf, qbuf, gsem, qsem):
    k = r_ref.shape[0]
    rows = green_ref.shape[0]
    nblk = k // NB
    get = pltpu.make_async_copy(green_ref, gbuf, gsem)
    get.start()
    a[...] = jnp.zeros_like(a)
    w[...] = jnp.zeros_like(w)
    blocks = upper_blocks(k)
    for i, (p, q) in enumerate(blocks):
        a[p * NB:(p + 1) * NB, q * NB:(q + 1) * NB] = sum_ref[i * NB:(i + 1) * NB, :]
    rhs = jnp.concatenate([sum_ref[RHS_AT + i:RHS_AT + i + 1, :RHS_W] for i in range(k // RHS_W)], axis=1)
    ri = lax.broadcasted_iota(jnp.int32, (NB, NB), 0)
    ci = lax.broadcasted_iota(jnp.int32, (NB, NB), 1)
    eye = jnp.where(ri == ci, 1.0, 0.0)
    corner = a[:NB, :NB]
    a[:NB, :NB] = jnp.where((ri >= RHS_AT) & (ci < RHS_W), jnp.transpose(corner), corner)

    def panel(p, carry):
        first = pl.multiple_of(p * NB, NB)
        at = pl.ds(first, NB)
        d = [a[pl.ds(first + SB * i, SB), at] for i in range(NB // SB)]
        v = [eye[SB * i:SB * i + SB] for i in range(NB // SB)]
        d, v = factor_block(d, v)
        dd = jnp.concatenate(d, axis=0)
        scale = lax.rsqrt(jnp.sum(jnp.where(ri == ci, dd, 0.0), axis=1, keepdims=True))
        a[at, at] = jnp.where(ri <= ci, dd * scale, 0.0)
        w[at, at] = jnp.where(ri >= ci, jnp.concatenate(v, axis=0) * scale, 0.0)
        for s in range(nblk):
            @pl.when(p == s)
            def _():
                lo, hi = s * NB, (s + 1) * NB
                inv = w[lo:hi, lo:hi]
                right = k - hi
                parts = ([a[lo:hi, hi:]] if right else []) + ([w[lo:hi, :lo]] if s else [])
                line = dot_hi(inv, jnp.concatenate(parts, axis=1) if len(parts) > 1 else parts[0], 1, 0)
                if s:
                    w[lo:hi, :lo] = line[:, right:]
                if right:
                    u = line[:, :right]
                    a[lo:hi, hi:] = u
                    move = dot_hi(u, jnp.concatenate([line, inv], axis=1), 0, 0)
                    a[hi:, hi:] = a[hi:, hi:] - move[:, :right]
                    w[hi:, :hi] = w[hi:, :hi] - move[:, right:]
        return carry

    lax.fori_loop(0, nblk, panel, 0)
    for p in range(1, nblk):
        a[p * NB:(p + 1) * NB, :p * NB] = jnp.zeros((NB, p * NB), jnp.float32)
    r_ref[...] = a[...] * (1.0 / rows_total ** 0.5)
    z_ref[...] = dot_hi(rhs, w[...], 1, 1)
    inv_high, inv_low = split(w[...] * (rows_total ** 0.5))
    get.wait()

    def q_out(t):
        at = slice(t * tile, (t + 1) * tile)
        return pltpu.make_async_copy(qbuf.at[at, :], q_ref.at[at, :], qsem.at[t])

    def dot_n(left, right):
        return lax.dot_general(left, right, (((1,), (1,)), ((), ())), preferred_element_type=jnp.float32)

    for t in range(rows // tile):
        at = slice(t * tile, (t + 1) * tile)
        high, low = split(gbuf[at, :])
        qbuf[at, :] = dot_n(high, inv_high) + (dot_n(low, inv_high) + dot_n(high, inv_low))
        q_out(t).start()
    for t in range(rows // tile):
        q_out(t).wait()


def factor_call(gram_sum, green, rows_total):
    rows, k = green.shape
    tile = 512
    vmem = pl.BlockSpec(memory_space=pltpu.VMEM)
    anywhere = pl.BlockSpec(memory_space=pl.ANY)
    f32 = jnp.float32
    return pl.pallas_call(
        functools.partial(factor_kernel, rows_total, tile),
        out_shape=(jax.ShapeDtypeStruct((k, k), f32), jax.ShapeDtypeStruct((1, k), f32), jax.ShapeDtypeStruct((rows, k), f32)),
        in_specs=[vmem, anywhere],
        out_specs=(vmem, vmem, anywhere),
        scratch_shapes=[
            pltpu.VMEM((k, k), f32), pltpu.VMEM((k, k), f32),
            pltpu.VMEM((rows, k), f32), pltpu.VMEM((rows, k), f32),
            pltpu.SemaphoreType.DMA, pltpu.SemaphoreType.DMA((rows // tile,)),
        ],
        name="factor",
        compiler_params=pltpu.CompilerParams(vmem_limit_bytes=60 << 20),
    )(gram_sum, green)


def on_device(coef, basis_idx, basis_w, owner_blocks, data, panel_live):
    green, gram_sum = green_call(coef, basis_idx, basis_w, owner_blocks, data, panel_live)
    rows_total = green.shape[0] * lax.axis_size("dev") * lax.axis_size("grp")
    r_factor, projected, q_rows = factor_call(gram_sum, green, rows_total)
    return (r_factor, projected.reshape(-1), q_rows)


def solution(mesh):
    in_specs = (P("dev", "grp"), P(), P(), P(), P(("grp", "dev")), P(("grp", "dev")))
    out_specs = (P(), P(), P(("grp", "dev"), None))
    return jax.shard_map(
        on_device, mesh=mesh, in_specs=in_specs, out_specs=out_specs, check_vma=False
    )
```

```python
import functools

import jax
import jax.numpy as jnp
from jax import lax
from jax.experimental import pallas as pl
from jax.experimental.pallas import tpu as pltpu
from jax.sharding import PartitionSpec as P

HI = lax.Precision.HIGHEST
MESH = pl.DeviceIdType.MESH
NB = 128
SB = 8
STRIP = 8
CHUNK = 256
BLK = 8
NY, NX, NC, NZ = 4, 4, 2, 4
NCHIP = NY * NX
NDEV = NCHIP * NC
PIECE = 40
HALF = NCHIP * PIECE
RHS_AT = 120
RHS_W = 64


def hops(oy, ox):
    return min(oy, NY - oy) + min(ox, NX - ox)


def peer_offsets():
    offs = [(oy, ox, oc) for oy in range(NY) for ox in range(NX) for oc in range(NC)]
    return sorted(offs[1:], key=lambda o: hops(o[0], o[1]))


def chip_offsets():
    offs = [(oy, ox) for oy in range(NY) for ox in range(NX)][1:]
    return sorted(offs, key=lambda o: -hops(o[0], o[1]))


def upper_blocks(k):
    n = k // NB
    return [(p, q) for p in range(n) for q in range(p, n)]


def dot_t(a, b):
    return lax.dot_general(a, b, (((0,), (0,)), ((), ())), preferred_element_type=jnp.float32)


def split(x):
    high = x.astype(jnp.bfloat16)
    return high, (x - high.astype(jnp.float32)).astype(jnp.bfloat16)


def green_kernel(
    owner_ref, live_ref, coef_ref, idx_hbm, w_hbm, data_ref,
    green_ref, sum_ref,
    panel, basis, gbuf, idx_ref, w_ref, rhs, packed, half, from_core, from_chip, from_z, total, load,
    send_a, recv_a, local_a, out_g, send_c, recv_c, send_p, recv_p, send_z, recv_z, send_g, recv_g, send_f, recv_f,
):
    rows = green_ref.shape[0]
    k = green_ref.shape[1]
    depth = coef_ref.shape[0]
    chunks = rows // CHUNK
    z, me = lax.axis_index("grp"), lax.axis_index("dev")
    c, x, y = me % NC, (me // NC) % NX, me // (NC * NX)
    chip = y * NX + x
    partner = chip * NC + (1 - c)
    peers = peer_offsets()
    chips = chip_offsets()

    def device_at(oy, ox, oc):
        return (lax.rem(y + oy, NY) * NX + lax.rem(x + ox, NX)) * NC + lax.rem(c + oc, NC)

    loads = [pltpu.make_async_copy(idx_hbm, idx_ref, load.at[0]), pltpu.make_async_copy(w_hbm, w_ref, load.at[1])]
    for one in loads:
        one.start()

    barrier = pltpu.get_barrier_semaphore()
    for off in peers:
        pl.semaphore_signal(barrier, inc=1, device_id=(z, device_at(*off)), device_id_type=MESH)
    for oz in range(1, NZ):
        pl.semaphore_signal(barrier, inc=1, device_id=(lax.rem(z + oz, NZ), me), device_id_type=MESH)
    pl.semaphore_wait(barrier, len(peers) + NZ - 1)

    def coef_copy(ch, i):
        to = device_at(*peers[i])
        at = pl.ds(pl.multiple_of(to * rows + ch * CHUNK, NB), CHUNK)
        return pltpu.make_async_remote_copy(
            src_ref=coef_ref.at[:, at], dst_ref=panel.at[ch, me],
            send_sem=send_a.at[ch, i], recv_sem=recv_a.at[ch, i],
            device_id=(z, to), device_id_type=MESH,
        )

    def own_copy(ch):
        at = pl.ds(pl.multiple_of(me * rows + ch * CHUNK, NB), CHUNK)
        return pltpu.make_async_copy(coef_ref.at[:, at], panel.at[ch, me], local_a.at[ch])

    def start_chunk(ch, carry):
        own_copy(ch).start()
        for i in range(len(peers)):
            coef_copy(ch, i).start()
        return carry

    lax.fori_loop(0, chunks, start_chunk, 0)

    group = 4
    slots = idx_ref.shape[0]

    def build(step, carry):
        parts = [jnp.zeros((BLK, k), jnp.float32) for _ in range(group)]
        owners = [owner_ref[step * group + i] for i in range(group)]
        for t in range(slots):
            ids = jnp.broadcast_to(idx_ref[t:t + 1, :], (BLK, k))
            weights = w_ref[t]
            for i in range(group):
                parts[i] = parts[i] + jnp.where(ids == owners[i], weights, 0.0)
        at = pl.ds(pl.multiple_of(step * group * BLK, group * BLK), group * BLK)
        basis[at, :] = jnp.concatenate(parts, axis=0).astype(jnp.bfloat16)
        return carry

    for one in loads:
        one.wait()
    lax.fori_loop(0, basis.shape[0] // (group * BLK), build, 0)

    blocks = upper_blocks(k)
    packed[...] = jnp.zeros_like(packed)
    rhs[...] = jnp.zeros_like(rhs)

    def green_out(ch):
        at = pl.ds(pl.multiple_of(ch * CHUNK, CHUNK), CHUNK)
        return pltpu.make_async_copy(gbuf.at[at, :], green_ref.at[at, :], out_g.at[ch])

    def work_chunk(ch, carry):
        own_copy(ch).wait()
        for i in range(len(peers)):
            coef_copy(ch, i).wait_recv()

        @pl.when(ch > 0)
        def _():
            for i in range(len(peers)):
                coef_copy(ch - 1, i).wait_send()

        block = panel[ch].reshape(NDEV * depth, CHUNK)
        green = dot_t(block, basis[...])
        row = lax.broadcasted_iota(jnp.int32, (CHUNK, k), 0) + ch * CHUNK
        green = jnp.where(row < live_ref[0], green, 0.0)
        at = pl.ds(pl.multiple_of(ch * CHUNK, CHUNK), CHUNK)
        gbuf[at, :] = green
        green_out(ch).start()
        high, low = split(green)
        gram = dot_t(high, high) + (dot_t(high, low) + dot_t(low, high))
        for i, (p, q) in enumerate(blocks):
            packed[i * NB:(i + 1) * NB, :] += gram[p * NB:(p + 1) * NB, q * NB:(q + 1) * NB]
        line = jnp.broadcast_to(data_ref[:, at], (SB, CHUNK))
        column = jnp.transpose(line)[:, :1]
        rhs[...] += jnp.sum((green * column).reshape(CHUNK // SB, SB, k), axis=0)
        return carry

    lax.fori_loop(0, chunks, work_chunk, 0)

    rhs_row = jnp.sum(rhs[...], axis=0, keepdims=True)
    for i in range(k // RHS_W):
        packed[RHS_AT + i:RHS_AT + i + 1, :RHS_W] = rhs_row[:, i * RHS_W:(i + 1) * RHS_W]

    def chip_at(oy, ox):
        return lax.rem(y + oy, NY) * NX + lax.rem(x + ox, NX)

    band = NX * PIECE

    def core_copy(oy):
        at = lax.rem(y + oy, NY) * band
        return pltpu.make_async_remote_copy(
            src_ref=packed.at[pl.ds(pl.multiple_of((1 - c) * HALF + at, SB), band), :],
            dst_ref=from_core.at[pl.ds(pl.multiple_of(at, SB), band), :],
            send_sem=send_c.at[oy], recv_sem=recv_c.at[oy],
            device_id=(z, partner), device_id_type=MESH,
        )

    def piece_copy(i):
        to = chip_at(*chips[i])
        return pltpu.make_async_remote_copy(
            src_ref=half.at[pl.ds(pl.multiple_of(to * PIECE, SB), PIECE), :], dst_ref=from_chip.at[i],
            send_sem=send_p.at[i], recv_sem=recv_p.at[i],
            device_id=(z, to * NC + c), device_id_type=MESH,
        )

    bands = (2, 1, 3, 0)
    for oy in bands:
        core_copy(oy).start()
    for oy in bands:
        core_copy(oy).wait_recv()
        at = lax.rem(y + oy, NY) * band
        here = pl.ds(pl.multiple_of(at, SB), band)
        half[here, :] = packed[pl.ds(pl.multiple_of(c * HALF + at, SB), band), :] + from_core[here, :]
        for i in range(len(chips)):
            if chips[i][0] == oy:
                piece_copy(i).start()
    part = half[pl.ds(pl.multiple_of(chip * PIECE, SB), PIECE), :]
    for i in reversed(range(len(chips))):
        piece_copy(i).wait_recv()
        part = part + from_chip[i]
    from_z[z] = part

    def z_copy(oz):
        return pltpu.make_async_remote_copy(
            src_ref=from_z.at[z], dst_ref=from_z.at[z], send_sem=send_z.at[oz - 1], recv_sem=recv_z.at[oz - 1],
            device_id=(lax.rem(z + oz, NZ), me), device_id_type=MESH,
        )

    for oz in (2, 1, 3):
        z_copy(oz).start()
    for oz in (1, 3, 2):
        z_copy(oz).wait_recv()

    def piece_of(chip_id):
        return pl.ds(pl.multiple_of(c * HALF + chip_id * PIECE, SB), PIECE)

    total[piece_of(chip), :] = (from_z[0] + from_z[1]) + (from_z[2] + from_z[3])

    def gather_copy(i):
        to = chip_at(*chips[i])
        return pltpu.make_async_remote_copy(
            src_ref=total.at[piece_of(chip), :], dst_ref=total.at[piece_of(chip), :],
            send_sem=send_g.at[i], recv_sem=recv_g.at[i],
            device_id=(z, to * NC + c), device_id_type=MESH,
        )

    def pass_on(chip_id, i):
        return pltpu.make_async_remote_copy(
            src_ref=total.at[piece_of(chip_id), :], dst_ref=total.at[piece_of(chip_id), :],
            send_sem=send_f.at[i], recv_sem=recv_f.at[i],
            device_id=(z, partner), device_id_type=MESH,
        )

    last = len(chips)
    for i in range(last):
        gather_copy(i).start()
    pass_on(chip, last).start()
    for i in reversed(range(last)):
        oy, ox = chips[i]
        gather_copy(i).wait_recv()
        pass_on(chip_at(NY - oy, NX - ox), i).start()
    for i in range(last + 1):
        pass_on(chip, i).wait()
    sum_ref[...] = total[...]

    for oy in bands:
        core_copy(oy).wait_send()
    for i in range(last):
        piece_copy(i).wait_send()
        gather_copy(i).wait_send()
    for oz in range(1, NZ):
        z_copy(oz).wait_send()

    def finish(ch, carry):
        green_out(ch).wait()
        return carry

    lax.fori_loop(0, chunks, finish, 0)
    for i in range(len(peers)):
        coef_copy(chunks - 1, i).wait_send()


def green_call(coef, basis_idx, basis_w, owner_blocks, data, panel_live):
    depth = coef.shape[0]
    rows = data.shape[0]
    k = basis_idx.shape[1]
    chunks = rows // CHUNK
    peers, chips = NDEV - 1, NCHIP - 1
    vmem = pl.BlockSpec(memory_space=pltpu.VMEM)
    smem = pl.BlockSpec(memory_space=pltpu.SMEM)
    anywhere = pl.BlockSpec(memory_space=pl.ANY)
    dma = pltpu.SemaphoreType.DMA
    f32 = jnp.float32
    return pl.pallas_call(
        green_kernel,
        out_shape=(jax.ShapeDtypeStruct((rows, k), f32), jax.ShapeDtypeStruct((2 * HALF, NB), f32)),
        in_specs=[smem, smem, anywhere, anywhere, anywhere, vmem],
        out_specs=(anywhere, vmem),
        scratch_shapes=[
            pltpu.VMEM((chunks, NDEV, depth, CHUNK), jnp.bfloat16),
            pltpu.VMEM((NDEV * depth, k), jnp.bfloat16),
            pltpu.VMEM((rows, k), f32),
            pltpu.VMEM(basis_idx.shape, jnp.int32),
            pltpu.VMEM(basis_w.shape, f32),
            pltpu.VMEM((SB, k), f32),
            pltpu.VMEM((2 * HALF, NB), f32),
            pltpu.VMEM((HALF, NB), f32),
            pltpu.VMEM((HALF, NB), f32),
            pltpu.VMEM((chips, PIECE, NB), f32),
            pltpu.VMEM((NZ, PIECE, NB), f32),
            pltpu.VMEM((2 * HALF, NB), f32),
            dma((2,)), dma((chunks, peers)), dma((chunks, peers)), dma((chunks,)), dma((chunks,)),
            dma((NY,)), dma((NY,)), dma((chips,)), dma((chips,)), dma((NZ - 1,)), dma((NZ - 1,)),
            dma((chips,)), dma((chips,)), dma((chips + 1,)), dma((chips + 1,)),
        ],
        name="green",
        compiler_params=pltpu.CompilerParams(collective_id=0, has_side_effects=True, vmem_limit_bytes=56 << 20),
    )(owner_blocks, panel_live, coef, basis_idx, basis_w, data.reshape(1, rows))


def dot_hi(a, b, ca, cb):
    return lax.dot_general(a, b, (((ca,), (cb,)), ((), ())), precision=HI, preferred_element_type=jnp.float32)


def dot_3(a, b, ca, cb):
    a_high, a_low = split(a)
    b_high, b_low = split(b)

    def one(left, right):
        return lax.dot_general(left, right, (((ca,), (cb,)), ((), ())), preferred_element_type=jnp.float32)

    return one(a_high, b_high) + (one(a_low, b_high) + one(a_high, b_low))


def factor_block(d, v):
    n = len(d)
    sub = lax.broadcasted_iota(jnp.int32, (SB, NB), 0)

    def bc(part):
        return jnp.broadcast_to(part, (SB, NB))

    for g0 in range(0, n, STRIP):
        scaled = []
        for g in range(g0, g0 + STRIP):
            j0 = SB * g
            def take(i):
                return [bc(d[i][:, j0 + c:j0 + c + 1]) for c in range(SB)]
            cols = take(g)
            steps = []
            iv = None
            for c in range(0, SB, 2):
                e = c + 1
                first = [bc(cols[x][c:e, :]) for x in range(c, SB)]
                second = [bc(cols[x][e:e + 1, :]) for x in range(e, SB)]
                pa, pb, pc = first[0], first[1], second[0]
                rdet = 1.0 / (pa * pc - pb * pb)
                inva = 1.0 / pa
                ka, kb, kc = pa * rdet, pb * rdet, pc * rdet
                pd0, pd1 = bc(d[g][c:e, :]), bc(d[g][e:e + 1, :])
                pv0, pv1 = bc(v[g][c:e, :]), bc(v[g][e:e + 1, :])
                rest = ((first[x - c], second[x - e], x) for x in range(e + 1, SB))
                step = (c, ka, kb, kc, list(rest), pd0, pd1, pv0, pv1)
                steps.append(step)
                u = cols[c] * kc - cols[e] * kb
                t = cols[e] * ka - cols[c] * kb
                u = jnp.where(sub > e, u, jnp.where(sub == e, pb * inva, 0.0))
                t = jnp.where(sub > e, t, 0.0)
                for f, s, x in step[4]:
                    cols[x] = cols[x] - (u * f + t * s)
                d[g] = d[g] - (u * pd0 + t * pd1)
                v[g] = v[g] - (u * pv0 + t * pv1)
                iv = inva if iv is None else jnp.where(sub == c, inva, iv)
                iv = jnp.where(sub == e, ka, iv)
            scaled.append(d[g] * iv)
            for i in range(g + 1, g0 + STRIP):
                cc = take(i)
                for c, ka, kb, kc, rest, pd0, pd1, pv0, pv1 in steps:
                    e = c + 1
                    u = cc[c] * kc - cc[e] * kb
                    t = cc[e] * ka - cc[c] * kb
                    for f, s, x in rest:
                        cc[x] = cc[x] - (u * f + t * s)
                    d[i] = d[i] - (u * pd0 + t * pd1)
                    v[i] = v[i] - (u * pv0 + t * pv1)
        g1 = g0 + STRIP
        if g1 < n:
            left = jnp.concatenate(scaled, axis=0)[:, SB * g1:]
            right = jnp.concatenate([jnp.concatenate(d[g0:g1], axis=0), jnp.concatenate(v[g0:g1], axis=0)], axis=1)
            mv = dot_hi(left, right, 0, 0)
            for i in range(g1, n):
                o = SB * (i - g1)
                d[i] = d[i] - mv[o:o + SB, :NB]
                v[i] = v[i] - mv[o:o + SB, NB:]
    return d, v


def factor_kernel(rows_total, tile, sum_ref, green_ref, r_ref, z_ref, q_ref, a, w, gbuf, qbuf, gsem, qsem):
    k = r_ref.shape[0]
    rows = green_ref.shape[0]
    nblk = k // NB
    get = pltpu.make_async_copy(green_ref, gbuf, gsem)
    get.start()
    a[...] = jnp.zeros_like(a)
    w[...] = jnp.zeros_like(w)
    blocks = upper_blocks(k)
    for i, (p, q) in enumerate(blocks):
        a[p * NB:(p + 1) * NB, q * NB:(q + 1) * NB] = sum_ref[i * NB:(i + 1) * NB, :]
    rhs = jnp.concatenate([sum_ref[RHS_AT + i:RHS_AT + i + 1, :RHS_W] for i in range(k // RHS_W)], axis=1)
    ri = lax.broadcasted_iota(jnp.int32, (NB, NB), 0)
    ci = lax.broadcasted_iota(jnp.int32, (NB, NB), 1)
    eye = jnp.where(ri == ci, 1.0, 0.0)
    corner = a[:NB, :NB]
    a[:NB, :NB] = jnp.where((ri >= RHS_AT) & (ci < RHS_W), jnp.transpose(corner), corner)

    def panel(p, carry):
        first = pl.multiple_of(p * NB, NB)
        at = pl.ds(first, NB)
        d = [a[pl.ds(first + SB * i, SB), at] for i in range(NB // SB)]
        v = [eye[SB * i:SB * i + SB] for i in range(NB // SB)]
        d, v = factor_block(d, v)
        dd = jnp.concatenate(d, axis=0)
        scale = lax.rsqrt(jnp.sum(jnp.where(ri == ci, dd, 0.0), axis=1, keepdims=True))
        a[at, at] = jnp.where(ri <= ci, dd * scale, 0.0)
        w[at, at] = jnp.where(ri >= ci, jnp.concatenate(v, axis=0) * scale, 0.0)
        for s in range(nblk):
            @pl.when(p == s)
            def _():
                lo, hi = s * NB, (s + 1) * NB
                inv = w[lo:hi, lo:hi]
                right = k - hi
                parts = ([a[lo:hi, hi:]] if right else []) + ([w[lo:hi, :lo]] if s else [])
                line = dot_3(inv, jnp.concatenate(parts, axis=1) if len(parts) > 1 else parts[0], 1, 0)
                if s:
                    w[lo:hi, :lo] = line[:, right:]
                if right:
                    u = line[:, :right]
                    a[lo:hi, hi:] = u
                    move = dot_3(u, jnp.concatenate([line, inv], axis=1), 0, 0)
                    a[hi:, hi:] = a[hi:, hi:] - move[:, :right]
                    w[hi:, :hi] = w[hi:, :hi] - move[:, right:]
        return carry

    lax.fori_loop(0, nblk, panel, 0)
    for p in range(1, nblk):
        a[p * NB:(p + 1) * NB, :p * NB] = jnp.zeros((NB, p * NB), jnp.float32)
    r_ref[...] = a[...] * (1.0 / rows_total ** 0.5)
    inv_high, inv_low = split(w[...] * (rows_total ** 0.5))

    def q_out(t):
        at = slice(t * tile, (t + 1) * tile)
        return pltpu.make_async_copy(qbuf.at[at, :], q_ref.at[at, :], qsem.at[t])

    def dot_n(left, right):
        return lax.dot_general(left, right, (((1,), (1,)), ((), ())), preferred_element_type=jnp.float32)

    wide = 2 * NB
    rhs_high, rhs_low = split(jnp.broadcast_to(rhs, (SB, k)))
    z = dot_n(rhs_high, inv_high) + (dot_n(rhs_low, inv_high) + dot_n(rhs_high, inv_low))
    z_ref[...] = z[:1] * (1.0 / rows_total ** 0.5)
    get.wait()
    for t in range(rows // tile):
        at = slice(t * tile, (t + 1) * tile)
        high, low = split(gbuf[at, :])
        for n0 in range(0, k, wide):
            n1 = n0 + wide
            right_high, right_low = inv_high[n0:n1, :n1], inv_low[n0:n1, :n1]
            left_high, left_low = high[:, :n1], low[:, :n1]
            qbuf[at, n0:n1] = dot_n(left_high, right_high) + (dot_n(left_low, right_high) + dot_n(left_high, right_low))
        q_out(t).start()
    for t in range(rows // tile):
        q_out(t).wait()


def factor_call(gram_sum, green, rows_total):
    rows, k = green.shape
    tile = 512
    vmem = pl.BlockSpec(memory_space=pltpu.VMEM)
    anywhere = pl.BlockSpec(memory_space=pl.ANY)
    f32 = jnp.float32
    return pl.pallas_call(
        functools.partial(factor_kernel, rows_total, tile),
        out_shape=(jax.ShapeDtypeStruct((k, k), f32), jax.ShapeDtypeStruct((1, k), f32), jax.ShapeDtypeStruct((rows, k), f32)),
        in_specs=[vmem, anywhere],
        out_specs=(vmem, vmem, anywhere),
        scratch_shapes=[
            pltpu.VMEM((k, k), f32), pltpu.VMEM((k, k), f32),
            pltpu.VMEM((rows, k), f32), pltpu.VMEM((rows, k), f32),
            pltpu.SemaphoreType.DMA, pltpu.SemaphoreType.DMA((rows // tile,)),
        ],
        name="factor",
        compiler_params=pltpu.CompilerParams(vmem_limit_bytes=60 << 20),
    )(gram_sum, green)


def on_device(coef, basis_idx, basis_w, owner_blocks, data, panel_live):
    green, gram_sum = green_call(coef, basis_idx, basis_w, owner_blocks, data, panel_live)
    rows_total = green.shape[0] * lax.axis_size("dev") * lax.axis_size("grp")
    r_factor, projected, q_rows = factor_call(gram_sum, green, rows_total)
    return (r_factor, projected.reshape(-1), q_rows)


def solution(mesh):
    in_specs = (P("dev", "grp"), P(), P(), P(), P(("grp", "dev")), P(("grp", "dev")))
    out_specs = (P(), P(), P(("grp", "dev"), None))
    return jax.shard_map(
        on_device, mesh=mesh, in_specs=in_specs, out_specs=out_specs, check_vma=False
    )
```

```python
import functools

import jax
import jax.numpy as jnp
from jax import lax
from jax.experimental import pallas as pl
from jax.experimental.pallas import tpu as pltpu
from jax.sharding import PartitionSpec as P

HI = lax.Precision.HIGHEST
MESH = pl.DeviceIdType.MESH
NB = 128
SB = 8
STRIP = 8
CHUNK = 256
BLK = 8
NY, NX, NC, NZ = 4, 4, 2, 4
NCHIP = NY * NX
NDEV = NCHIP * NC
PIECE = 40
HALF = NCHIP * PIECE
RHS_AT = 120
RHS_W = 64


def hops(oy, ox):
    return min(oy, NY - oy) + min(ox, NX - ox)


def peer_offsets():
    offs = [(oy, ox, oc) for oy in range(NY) for ox in range(NX) for oc in range(NC)]
    return sorted(offs[1:], key=lambda o: hops(o[0], o[1]))


def chip_offsets():
    offs = [(oy, ox) for oy in range(NY) for ox in range(NX)][1:]
    return sorted(offs, key=lambda o: -hops(o[0], o[1]))


def upper_blocks(k):
    n = k // NB
    return [(p, q) for p in range(n) for q in range(p, n)]


def dot_t(a, b):
    return lax.dot_general(a, b, (((0,), (0,)), ((), ())), preferred_element_type=jnp.float32)


def split(x):
    high = x.astype(jnp.bfloat16)
    return high, (x - high.astype(jnp.float32)).astype(jnp.bfloat16)


def green_kernel(
    owner_ref, live_ref, coef_ref, idx_hbm, w_hbm, data_ref,
    green_ref, sum_ref,
    panel, basis, gbuf, idx_ref, w_ref, rhs, packed, half, from_core, from_chip, from_z, total, load,
    send_a, recv_a, local_a, out_g, send_c, recv_c, send_p, recv_p, send_z, recv_z, send_g, recv_g, send_f, recv_f,
):
    rows = green_ref.shape[0]
    k = green_ref.shape[1]
    depth = coef_ref.shape[0]
    chunks = rows // CHUNK
    z, me = lax.axis_index("grp"), lax.axis_index("dev")
    c, x, y = me % NC, (me // NC) % NX, me // (NC * NX)
    chip = y * NX + x
    partner = chip * NC + (1 - c)
    peers = peer_offsets()
    chips = chip_offsets()

    def device_at(oy, ox, oc):
        return (lax.rem(y + oy, NY) * NX + lax.rem(x + ox, NX)) * NC + lax.rem(c + oc, NC)

    loads = [pltpu.make_async_copy(idx_hbm, idx_ref, load.at[0]), pltpu.make_async_copy(w_hbm, w_ref, load.at[1])]
    for one in loads:
        one.start()

    barrier = pltpu.get_barrier_semaphore()
    for off in reversed(peers):
        pl.semaphore_signal(barrier, inc=1, device_id=(z, device_at(*off)), device_id_type=MESH)
    for oz in range(1, NZ):
        pl.semaphore_signal(barrier, inc=1, device_id=(lax.rem(z + oz, NZ), me), device_id_type=MESH)
    pl.semaphore_wait(barrier, len(peers) + NZ - 1)

    def coef_copy(ch, i):
        to = device_at(*peers[i])
        at = pl.ds(pl.multiple_of(to * rows + ch * CHUNK, NB), CHUNK)
        return pltpu.make_async_remote_copy(
            src_ref=coef_ref.at[:, at], dst_ref=panel.at[ch, me],
            send_sem=send_a.at[ch, i], recv_sem=recv_a.at[ch, i],
            device_id=(z, to), device_id_type=MESH,
        )

    def own_copy(ch):
        at = pl.ds(pl.multiple_of(me * rows + ch * CHUNK, NB), CHUNK)
        return pltpu.make_async_copy(coef_ref.at[:, at], panel.at[ch, me], local_a.at[ch])

    def start_chunk(ch, carry):
        own_copy(ch).start()
        for i in range(len(peers)):
            coef_copy(ch, i).start()
        return carry

    lax.fori_loop(0, chunks, start_chunk, 0)

    group = 4
    slots = idx_ref.shape[0]

    def build(step, carry):
        parts = [jnp.zeros((BLK, k), jnp.float32) for _ in range(group)]
        owners = [owner_ref[step * group + i] for i in range(group)]
        for t in range(slots):
            ids = jnp.broadcast_to(idx_ref[t:t + 1, :], (BLK, k))
            weights = w_ref[t]
            for i in range(group):
                parts[i] = parts[i] + jnp.where(ids == owners[i], weights, 0.0)
        at = pl.ds(pl.multiple_of(step * group * BLK, group * BLK), group * BLK)
        basis[at, :] = jnp.concatenate(parts, axis=0).astype(jnp.bfloat16)
        return carry

    for one in loads:
        one.wait()
    lax.fori_loop(0, basis.shape[0] // (group * BLK), build, 0)

    blocks = upper_blocks(k)
    packed[...] = jnp.zeros_like(packed)
    rhs[...] = jnp.zeros_like(rhs)

    def green_out(ch):
        at = pl.ds(pl.multiple_of(ch * CHUNK, CHUNK), CHUNK)
        return pltpu.make_async_copy(gbuf.at[at, :], green_ref.at[at, :], out_g.at[ch])

    def work_chunk(ch, carry):
        own_copy(ch).wait()
        for i in range(len(peers)):
            coef_copy(ch, i).wait_recv()

        @pl.when(ch < chunks - 1)
        def _():
            @pl.when(ch > 0)
            def _():
                for i in range(len(peers)):
                    coef_copy(ch - 1, i).wait_send()

        block = panel[ch].reshape(NDEV * depth, CHUNK)
        green = dot_t(block, basis[...])
        row = lax.broadcasted_iota(jnp.int32, (CHUNK, k), 0) + ch * CHUNK
        green = jnp.where(row < live_ref[0], green, 0.0)
        at = pl.ds(pl.multiple_of(ch * CHUNK, CHUNK), CHUNK)
        gbuf[at, :] = green
        green_out(ch).start()
        high, low = split(green)
        gram = dot_t(high, high) + (dot_t(high, low) + dot_t(low, high))
        for i, (p, q) in enumerate(blocks):
            packed[i * NB:(i + 1) * NB, :] += gram[p * NB:(p + 1) * NB, q * NB:(q + 1) * NB]
        line = jnp.broadcast_to(data_ref[:, at], (SB, CHUNK))
        column = jnp.transpose(line)[:, :1]
        rhs[...] += jnp.sum((green * column).reshape(CHUNK // SB, SB, k), axis=0)
        return carry

    lax.fori_loop(0, chunks, work_chunk, 0)

    rhs_row = jnp.sum(rhs[...], axis=0, keepdims=True)
    for i in range(k // RHS_W):
        packed[RHS_AT + i:RHS_AT + i + 1, :RHS_W] = rhs_row[:, i * RHS_W:(i + 1) * RHS_W]

    def chip_at(oy, ox):
        return lax.rem(y + oy, NY) * NX + lax.rem(x + ox, NX)

    band = NX * PIECE

    def core_copy(oy):
        at = lax.rem(y + oy, NY) * band
        return pltpu.make_async_remote_copy(
            src_ref=packed.at[pl.ds(pl.multiple_of((1 - c) * HALF + at, SB), band), :],
            dst_ref=from_core.at[pl.ds(pl.multiple_of(at, SB), band), :],
            send_sem=send_c.at[oy], recv_sem=recv_c.at[oy],
            device_id=(z, partner), device_id_type=MESH,
        )

    def piece_copy(i):
        to = chip_at(*chips[i])
        return pltpu.make_async_remote_copy(
            src_ref=half.at[pl.ds(pl.multiple_of(to * PIECE, SB), PIECE), :], dst_ref=from_chip.at[i],
            send_sem=send_p.at[i], recv_sem=recv_p.at[i],
            device_id=(z, to * NC + c), device_id_type=MESH,
        )

    bands = (2, 1, 3, 0)
    for oy in bands:
        core_copy(oy).start()
    for i in range(len(peers)):
        coef_copy(chunks - 2, i).wait_send()
    for oy in bands:
        core_copy(oy).wait_recv()
        at = lax.rem(y + oy, NY) * band
        here = pl.ds(pl.multiple_of(at, SB), band)
        half[here, :] = packed[pl.ds(pl.multiple_of(c * HALF + at, SB), band), :] + from_core[here, :]
        for i in range(len(chips)):
            if chips[i][0] == oy:
                piece_copy(i).start()
    for i in range(len(peers)):
        coef_copy(chunks - 1, i).wait_send()
    for oy in bands:
        core_copy(oy).wait_send()
    part = half[pl.ds(pl.multiple_of(chip * PIECE, SB), PIECE), :]
    for i in reversed(range(len(chips))):
        piece_copy(i).wait_recv()
        part = part + from_chip[i]
    from_z[z] = part

    def z_copy(oz):
        return pltpu.make_async_remote_copy(
            src_ref=from_z.at[z], dst_ref=from_z.at[z], send_sem=send_z.at[oz - 1], recv_sem=recv_z.at[oz - 1],
            device_id=(lax.rem(z + oz, NZ), me), device_id_type=MESH,
        )

    for oz in (2, 1, 3):
        z_copy(oz).start()

    def finish(ch, carry):
        green_out(ch).wait()
        return carry

    lax.fori_loop(0, chunks, finish, 0)
    for i in range(len(chips)):
        piece_copy(i).wait_send()
    for oz in (1, 3, 2):
        z_copy(oz).wait_recv()

    def piece_of(chip_id):
        return pl.ds(pl.multiple_of(c * HALF + chip_id * PIECE, SB), PIECE)

    total[piece_of(chip), :] = (from_z[0] + from_z[1]) + (from_z[2] + from_z[3])

    def gather_copy(i):
        to = chip_at(*chips[i])
        return pltpu.make_async_remote_copy(
            src_ref=total.at[piece_of(chip), :], dst_ref=total.at[piece_of(chip), :],
            send_sem=send_g.at[i], recv_sem=recv_g.at[i],
            device_id=(z, to * NC + c), device_id_type=MESH,
        )

    def pass_on(chip_id, i):
        return pltpu.make_async_remote_copy(
            src_ref=total.at[piece_of(chip_id), :], dst_ref=total.at[piece_of(chip_id), :],
            send_sem=send_f.at[i], recv_sem=recv_f.at[i],
            device_id=(z, partner), device_id_type=MESH,
        )

    last = len(chips)
    for i in range(last):
        gather_copy(i).start()
    pass_on(chip, last).start()
    for i in reversed(range(last)):
        oy, ox = chips[i]
        gather_copy(i).wait_recv()
        pass_on(chip_at(NY - oy, NX - ox), i).start()
    for i in range(last + 1):
        pass_on(chip, i).wait()
    sum_ref[...] = total[...]

    for i in range(last):
        gather_copy(i).wait_send()
    for oz in range(1, NZ):
        z_copy(oz).wait_send()


def green_call(coef, basis_idx, basis_w, owner_blocks, data, panel_live):
    depth = coef.shape[0]
    rows = data.shape[0]
    k = basis_idx.shape[1]
    chunks = rows // CHUNK
    peers, chips = NDEV - 1, NCHIP - 1
    vmem = pl.BlockSpec(memory_space=pltpu.VMEM)
    smem = pl.BlockSpec(memory_space=pltpu.SMEM)
    anywhere = pl.BlockSpec(memory_space=pl.ANY)
    dma = pltpu.SemaphoreType.DMA
    f32 = jnp.float32
    return pl.pallas_call(
        green_kernel,
        out_shape=(jax.ShapeDtypeStruct((rows, k), f32), jax.ShapeDtypeStruct((2 * HALF, NB), f32)),
        in_specs=[smem, smem, anywhere, anywhere, anywhere, vmem],
        out_specs=(anywhere, vmem),
        scratch_shapes=[
            pltpu.VMEM((chunks, NDEV, depth, CHUNK), jnp.bfloat16),
            pltpu.VMEM((NDEV * depth, k), jnp.bfloat16),
            pltpu.VMEM((rows, k), f32),
            pltpu.VMEM(basis_idx.shape, jnp.int32),
            pltpu.VMEM(basis_w.shape, f32),
            pltpu.VMEM((SB, k), f32),
            pltpu.VMEM((2 * HALF, NB), f32),
            pltpu.VMEM((HALF, NB), f32),
            pltpu.VMEM((HALF, NB), f32),
            pltpu.VMEM((chips, PIECE, NB), f32),
            pltpu.VMEM((NZ, PIECE, NB), f32),
            pltpu.VMEM((2 * HALF, NB), f32),
            dma((2,)), dma((chunks, peers)), dma((chunks, peers)), dma((chunks,)), dma((chunks,)),
            dma((NY,)), dma((NY,)), dma((chips,)), dma((chips,)), dma((NZ - 1,)), dma((NZ - 1,)),
            dma((chips,)), dma((chips,)), dma((chips + 1,)), dma((chips + 1,)),
        ],
        name="green",
        compiler_params=pltpu.CompilerParams(collective_id=0, has_side_effects=True, vmem_limit_bytes=56 << 20),
    )(owner_blocks, panel_live, coef, basis_idx, basis_w, data.reshape(1, rows))


def dot_hi(a, b, ca, cb):
    return lax.dot_general(a, b, (((ca,), (cb,)), ((), ())), precision=HI, preferred_element_type=jnp.float32)


def dot_3(a, b, ca, cb):
    a_high, a_low = split(a)
    b_high, b_low = split(b)

    def one(left, right):
        return lax.dot_general(left, right, (((ca,), (cb,)), ((), ())), preferred_element_type=jnp.float32)

    return one(a_high, b_high) + (one(a_low, b_high) + one(a_high, b_low))


def factor_block(d, v):
    n = len(d)
    sub = lax.broadcasted_iota(jnp.int32, (SB, NB), 0)

    def bc(part):
        return jnp.broadcast_to(part, (SB, NB))

    for g0 in range(0, n, STRIP):
        scaled = []
        for g in range(g0, g0 + STRIP):
            j0 = SB * g
            def take(i):
                return [bc(d[i][:, j0 + c:j0 + c + 1]) for c in range(SB)]
            cols = take(g)
            steps = []
            iv = None
            for c in range(0, SB, 2):
                e = c + 1
                first = [bc(cols[x][c:e, :]) for x in range(c, SB)]
                second = [bc(cols[x][e:e + 1, :]) for x in range(e, SB)]
                pa, pb, pc = first[0], first[1], second[0]
                rdet = 1.0 / (pa * pc - pb * pb)
                inva = 1.0 / pa
                ka, kb, kc = pa * rdet, pb * rdet, pc * rdet
                pd0, pd1 = bc(d[g][c:e, :]), bc(d[g][e:e + 1, :])
                pv0, pv1 = bc(v[g][c:e, :]), bc(v[g][e:e + 1, :])
                rest = ((first[x - c], second[x - e], x) for x in range(e + 1, SB))
                step = (c, ka, kb, kc, list(rest), pd0, pd1, pv0, pv1)
                steps.append(step)
                u = cols[c] * kc - cols[e] * kb
                t = cols[e] * ka - cols[c] * kb
                u = jnp.where(sub > e, u, jnp.where(sub == e, pb * inva, 0.0))
                t = jnp.where(sub > e, t, 0.0)
                for f, s, x in step[4]:
                    cols[x] = cols[x] - (u * f + t * s)
                d[g] = d[g] - (u * pd0 + t * pd1)
                v[g] = v[g] - (u * pv0 + t * pv1)
                iv = inva if iv is None else jnp.where(sub == c, inva, iv)
                iv = jnp.where(sub == e, ka, iv)
            scaled.append(d[g] * iv)
            for i in range(g + 1, g0 + STRIP):
                cc = take(i)
                for c, ka, kb, kc, rest, pd0, pd1, pv0, pv1 in steps:
                    e = c + 1
                    u = cc[c] * kc - cc[e] * kb
                    t = cc[e] * ka - cc[c] * kb
                    for f, s, x in rest:
                        cc[x] = cc[x] - (u * f + t * s)
                    d[i] = d[i] - (u * pd0 + t * pd1)
                    v[i] = v[i] - (u * pv0 + t * pv1)
        g1 = g0 + STRIP
        if g1 < n:
            left = jnp.concatenate(scaled, axis=0)[:, SB * g1:]
            right = jnp.concatenate([jnp.concatenate(d[g0:g1], axis=0), jnp.concatenate(v[g0:g1], axis=0)], axis=1)
            mv = dot_hi(left, right, 0, 0)
            for i in range(g1, n):
                o = SB * (i - g1)
                d[i] = d[i] - mv[o:o + SB, :NB]
                v[i] = v[i] - mv[o:o + SB, NB:]
    return d, v


def factor_kernel(rows_total, tile, sum_ref, green_ref, r_ref, z_ref, q_ref, a, w, corner, gbuf, qbuf, bsem, gsem, qsem):
    k = r_ref.shape[0]
    rows = green_ref.shape[0]
    nblk = k // NB
    blocks = upper_blocks(k)

    def block_in(i):
        p, q = blocks[i]
        to = corner if i == 0 else a.at[p * NB:(p + 1) * NB, q * NB:(q + 1) * NB]
        return pltpu.make_async_copy(sum_ref.at[i * NB:(i + 1) * NB, :], to, bsem.at[i])

    for i in range(len(blocks)):
        block_in(i).start()
    get = pltpu.make_async_copy(green_ref, gbuf, gsem)
    get.start()

    def clear_lower():
        for p in range(1, nblk):
            a[p * NB:(p + 1) * NB, :p * NB] = jnp.zeros((NB, p * NB), jnp.float32)

    clear_lower()
    w[...] = jnp.zeros_like(w)
    ri = lax.broadcasted_iota(jnp.int32, (NB, NB), 0)
    ci = lax.broadcasted_iota(jnp.int32, (NB, NB), 1)
    eye = jnp.where(ri == ci, 1.0, 0.0)
    block_in(0).wait()
    head = corner[...]
    rhs = jnp.concatenate([head[RHS_AT + i:RHS_AT + i + 1, :RHS_W] for i in range(k // RHS_W)], axis=1)
    a[:NB, :NB] = jnp.where((ri >= RHS_AT) & (ci < RHS_W), jnp.transpose(head), head)

    def panel(p, carry):
        first = pl.multiple_of(p * NB, NB)
        at = pl.ds(first, NB)
        d = [a[pl.ds(first + SB * i, SB), at] for i in range(NB // SB)]
        v = [eye[SB * i:SB * i + SB] for i in range(NB // SB)]
        d, v = factor_block(d, v)
        dd = jnp.concatenate(d, axis=0)
        scale = lax.rsqrt(jnp.sum(jnp.where(ri == ci, dd, 0.0), axis=1, keepdims=True))
        a[at, at] = jnp.where(ri <= ci, dd * scale, 0.0)
        w[at, at] = jnp.where(ri >= ci, jnp.concatenate(v, axis=0) * scale, 0.0)
        for s in range(nblk):
            @pl.when(p == s)
            def _():
                if s == 0:
                    for i in range(1, len(blocks)):
                        block_in(i).wait()
                lo, hi = s * NB, (s + 1) * NB
                inv = w[lo:hi, lo:hi]
                right = k - hi
                parts = ([a[lo:hi, hi:]] if right else []) + ([w[lo:hi, :lo]] if s else [])
                line = dot_3(inv, jnp.concatenate(parts, axis=1) if len(parts) > 1 else parts[0], 1, 0)
                if s:
                    w[lo:hi, :lo] = line[:, right:]
                if right:
                    u = line[:, :right]
                    a[lo:hi, hi:] = u
                    move = dot_3(u, jnp.concatenate([line, inv], axis=1), 0, 0)
                    a[hi:, hi:] = a[hi:, hi:] - move[:, :right]
                    w[hi:, :hi] = w[hi:, :hi] - move[:, right:]
        return carry

    lax.fori_loop(0, nblk, panel, 0)
    clear_lower()
    r_ref[...] = a[...] * (1.0 / rows_total ** 0.5)
    inv_high, inv_low = split(w[...] * (rows_total ** 0.5))

    def q_out(t):
        at = slice(t * tile, (t + 1) * tile)
        return pltpu.make_async_copy(qbuf.at[at, :], q_ref.at[at, :], qsem.at[t])

    def dot_n(left, right):
        return lax.dot_general(left, right, (((1,), (1,)), ((), ())), preferred_element_type=jnp.float32)

    wide = 2 * NB
    rhs_high, rhs_low = split(jnp.broadcast_to(rhs, (SB, k)))
    z = dot_n(rhs_high, inv_high) + (dot_n(rhs_low, inv_high) + dot_n(rhs_high, inv_low))
    z_ref[...] = z[:1] * (1.0 / rows_total ** 0.5)
    get.wait()
    for t in range(rows // tile):
        at = slice(t * tile, (t + 1) * tile)
        high, low = split(gbuf[at, :])
        for n0 in range(0, k, wide):
            n1 = n0 + wide
            right_high, right_low = inv_high[n0:n1, :n1], inv_low[n0:n1, :n1]
            left_high, left_low = high[:, :n1], low[:, :n1]
            qbuf[at, n0:n1] = dot_n(left_high, right_high) + (dot_n(left_low, right_high) + dot_n(left_high, right_low))
        q_out(t).start()
    for t in range(rows // tile):
        q_out(t).wait()


def factor_call(gram_sum, green, rows_total):
    rows, k = green.shape
    tile = 512
    vmem = pl.BlockSpec(memory_space=pltpu.VMEM)
    anywhere = pl.BlockSpec(memory_space=pl.ANY)
    f32 = jnp.float32
    return pl.pallas_call(
        functools.partial(factor_kernel, rows_total, tile),
        out_shape=(jax.ShapeDtypeStruct((k, k), f32), jax.ShapeDtypeStruct((1, k), f32), jax.ShapeDtypeStruct((rows, k), f32)),
        in_specs=[anywhere, anywhere],
        out_specs=(vmem, vmem, anywhere),
        scratch_shapes=[
            pltpu.VMEM((k, k), f32), pltpu.VMEM((k, k), f32), pltpu.VMEM((NB, NB), f32),
            pltpu.VMEM((rows, k), f32), pltpu.VMEM((rows, k), f32),
            pltpu.SemaphoreType.DMA((len(upper_blocks(k)),)), pltpu.SemaphoreType.DMA, pltpu.SemaphoreType.DMA((rows // tile,)),
        ],
        name="factor",
        compiler_params=pltpu.CompilerParams(vmem_limit_bytes=60 << 20),
    )(gram_sum, green)


def on_device(coef, basis_idx, basis_w, owner_blocks, data, panel_live):
    green, gram_sum = green_call(coef, basis_idx, basis_w, owner_blocks, data, panel_live)
    rows_total = green.shape[0] * lax.axis_size("dev") * lax.axis_size("grp")
    r_factor, projected, q_rows = factor_call(gram_sum, green, rows_total)
    return (r_factor, projected.reshape(-1), q_rows)


def solution(mesh):
    in_specs = (P("dev", "grp"), P(), P(), P(), P(("grp", "dev")), P(("grp", "dev")))
    out_specs = (P(), P(), P(("grp", "dev"), None))
    return jax.shard_map(
        on_device, mesh=mesh, in_specs=in_specs, out_specs=out_specs, check_vma=False
    )
```

```python
import functools

import jax
import jax.numpy as jnp
from jax import lax
from jax.experimental import pallas as pl
from jax.experimental.pallas import tpu as pltpu
from jax.sharding import PartitionSpec as P

HI = lax.Precision.HIGHEST
MESH = pl.DeviceIdType.MESH
NB = 128
SB = 8
STRIP = 8
CHUNK = 256
BLK = 8
NY, NX, NC, NZ = 4, 4, 2, 4
NCHIP = NY * NX
NDEV = NCHIP * NC
PIECE = 40
HALF = NCHIP * PIECE
RHS_AT = 120
RHS_W = 64


def hops(oy, ox):
    return min(oy, NY - oy) + min(ox, NX - ox)


def peer_offsets():
    offs = [(oy, ox, oc) for oy in range(NY) for ox in range(NX) for oc in range(NC)]
    return sorted(offs[1:], key=lambda o: hops(o[0], o[1]))


def chip_offsets():
    offs = [(oy, ox) for oy in range(NY) for ox in range(NX)][1:]
    return sorted(offs, key=lambda o: -hops(o[0], o[1]))


def upper_blocks(k):
    n = k // NB
    return [(p, q) for p in range(n) for q in range(p, n)]


def dot_t(a, b):
    return lax.dot_general(a, b, (((0,), (0,)), ((), ())), preferred_element_type=jnp.float32)


def split(x):
    high = x.astype(jnp.bfloat16)
    return high, (x - high.astype(jnp.float32)).astype(jnp.bfloat16)


def green_kernel(
    owner_hbm, live_ref, coef_ref, idx_hbm, w_hbm, data_hbm,
    green_ref, sum_ref,
    panel, basis, gbuf, owner_ref, idx_ref, w_ref, data_ref, rhs, packed, half, from_core, from_chip, from_z, total, load,
    send_a, recv_a, local_a, out_g, send_c, recv_c, send_p, recv_p, send_z, recv_z, send_g, recv_g, send_f, recv_f,
):
    rows = green_ref.shape[0]
    k = green_ref.shape[1]
    depth = coef_ref.shape[0]
    chunks = rows // CHUNK
    z, me = lax.axis_index("grp"), lax.axis_index("dev")
    c, x, y = me % NC, (me // NC) % NX, me // (NC * NX)
    chip = y * NX + x
    partner = chip * NC + (1 - c)
    peers = peer_offsets()
    chips = chip_offsets()

    def device_at(oy, ox, oc):
        return (lax.rem(y + oy, NY) * NX + lax.rem(x + ox, NX)) * NC + lax.rem(c + oc, NC)

    pairs = ((idx_hbm, idx_ref), (w_hbm, w_ref), (data_hbm, data_ref), (owner_hbm, owner_ref))
    loads = [pltpu.make_async_copy(src, dst, load.at[i]) for i, (src, dst) in enumerate(pairs)]
    for one in loads:
        one.start()

    barrier = pltpu.get_barrier_semaphore()
    for off in reversed(peers):
        pl.semaphore_signal(barrier, inc=1, device_id=(z, device_at(*off)), device_id_type=MESH)
    for oz in range(1, NZ):
        pl.semaphore_signal(barrier, inc=1, device_id=(lax.rem(z + oz, NZ), me), device_id_type=MESH)
    pl.semaphore_wait(barrier, len(peers) + NZ - 1)

    def coef_copy(ch, i):
        to = device_at(*peers[i])
        at = pl.ds(pl.multiple_of(to * rows + ch * CHUNK, NB), CHUNK)
        return pltpu.make_async_remote_copy(
            src_ref=coef_ref.at[:, at], dst_ref=panel.at[ch, me],
            send_sem=send_a.at[ch, i], recv_sem=recv_a.at[ch, i],
            device_id=(z, to), device_id_type=MESH,
        )

    def own_copy(ch):
        at = pl.ds(pl.multiple_of(me * rows + ch * CHUNK, NB), CHUNK)
        return pltpu.make_async_copy(coef_ref.at[:, at], panel.at[ch, me], local_a.at[ch])

    def start_chunk(ch, carry):
        own_copy(ch).start()
        for i in range(len(peers)):
            coef_copy(ch, i).start()
        return carry

    lax.fori_loop(0, chunks, start_chunk, 0)

    group = 4
    slots = idx_ref.shape[0]

    def build(step, carry):
        parts = [jnp.zeros((BLK, k), jnp.float32) for _ in range(group)]
        owners = [owner_ref[step * group + i] for i in range(group)]
        for t in range(slots):
            ids = jnp.broadcast_to(idx_ref[t:t + 1, :], (BLK, k))
            weights = w_ref[t]
            for i in range(group):
                parts[i] = parts[i] + jnp.where(ids == owners[i], weights, 0.0)
        at = pl.ds(pl.multiple_of(step * group * BLK, group * BLK), group * BLK)
        basis[at, :] = jnp.concatenate(parts, axis=0).astype(jnp.bfloat16)
        return carry

    for one in loads:
        one.wait()
    lax.fori_loop(0, basis.shape[0] // (group * BLK), build, 0)

    blocks = upper_blocks(k)
    packed[...] = jnp.zeros_like(packed)
    rhs[...] = jnp.zeros_like(rhs)

    def green_out(ch):
        at = pl.ds(pl.multiple_of(ch * CHUNK, CHUNK), CHUNK)
        return pltpu.make_async_copy(gbuf.at[at, :], green_ref.at[at, :], out_g.at[ch])

    def work_chunk(ch, carry):
        own_copy(ch).wait()
        for i in range(len(peers)):
            coef_copy(ch, i).wait_recv()

        @pl.when(ch < chunks - 1)
        def _():
            @pl.when(ch > 0)
            def _():
                for i in range(len(peers)):
                    coef_copy(ch - 1, i).wait_send()

        block = panel[ch].reshape(NDEV * depth, CHUNK)
        green = dot_t(block, basis[...])
        row = lax.broadcasted_iota(jnp.int32, (CHUNK, k), 0) + ch * CHUNK
        green = jnp.where(row < live_ref[0], green, 0.0)
        at = pl.ds(pl.multiple_of(ch * CHUNK, CHUNK), CHUNK)
        high, low = split(green)
        gram = dot_t(high, high) + (dot_t(high, low) + dot_t(low, high))
        for i, (p, q) in enumerate(blocks):
            packed[i * NB:(i + 1) * NB, :] += gram[p * NB:(p + 1) * NB, q * NB:(q + 1) * NB]
        line = jnp.broadcast_to(data_ref[:, at], (SB, CHUNK))
        column = jnp.transpose(line)[:, :1]
        rhs[...] += jnp.sum((green * column).reshape(CHUNK // SB, SB, k), axis=0)
        gbuf[at, :] = green
        green_out(ch).start()
        return carry

    lax.fori_loop(0, chunks, work_chunk, 0)

    rhs_row = jnp.sum(rhs[...], axis=0, keepdims=True)
    for i in range(k // RHS_W):
        packed[RHS_AT + i:RHS_AT + i + 1, :RHS_W] = rhs_row[:, i * RHS_W:(i + 1) * RHS_W]

    def chip_at(oy, ox):
        return lax.rem(y + oy, NY) * NX + lax.rem(x + ox, NX)

    band = NX * PIECE

    def core_copy(oy):
        at = lax.rem(y + oy, NY) * band
        return pltpu.make_async_remote_copy(
            src_ref=packed.at[pl.ds(pl.multiple_of((1 - c) * HALF + at, SB), band), :],
            dst_ref=from_core.at[pl.ds(pl.multiple_of(at, SB), band), :],
            send_sem=send_c.at[oy], recv_sem=recv_c.at[oy],
            device_id=(z, partner), device_id_type=MESH,
        )

    def piece_copy(i):
        to = chip_at(*chips[i])
        return pltpu.make_async_remote_copy(
            src_ref=half.at[pl.ds(pl.multiple_of(to * PIECE, SB), PIECE), :], dst_ref=from_chip.at[i],
            send_sem=send_p.at[i], recv_sem=recv_p.at[i],
            device_id=(z, to * NC + c), device_id_type=MESH,
        )

    bands = (2, 1, 3, 0)
    for oy in bands:
        core_copy(oy).start()
    for i in range(len(peers)):
        coef_copy(chunks - 2, i).wait_send()
    for oy in bands:
        core_copy(oy).wait_recv()
        at = lax.rem(y + oy, NY) * band
        here = pl.ds(pl.multiple_of(at, SB), band)
        half[here, :] = packed[pl.ds(pl.multiple_of(c * HALF + at, SB), band), :] + from_core[here, :]
        for i in range(len(chips)):
            if chips[i][0] == oy:
                piece_copy(i).start()
    for i in range(len(peers)):
        coef_copy(chunks - 1, i).wait_send()
    for oy in bands:
        core_copy(oy).wait_send()
    part = half[pl.ds(pl.multiple_of(chip * PIECE, SB), PIECE), :]
    for i in reversed(range(len(chips))):
        piece_copy(i).wait_recv()
        part = part + from_chip[i]
    from_z[z] = part

    def z_copy(oz):
        return pltpu.make_async_remote_copy(
            src_ref=from_z.at[z], dst_ref=from_z.at[z], send_sem=send_z.at[oz - 1], recv_sem=recv_z.at[oz - 1],
            device_id=(lax.rem(z + oz, NZ), me), device_id_type=MESH,
        )

    for oz in (2, 1, 3):
        z_copy(oz).start()

    def finish(ch, carry):
        green_out(ch).wait()
        return carry

    lax.fori_loop(0, chunks, finish, 0)
    for i in range(len(chips)):
        piece_copy(i).wait_send()
    for oz in (1, 3, 2):
        z_copy(oz).wait_recv()

    def piece_of(chip_id):
        return pl.ds(pl.multiple_of(c * HALF + chip_id * PIECE, SB), PIECE)

    total[piece_of(chip), :] = (from_z[0] + from_z[1]) + (from_z[2] + from_z[3])

    def gather_copy(i):
        to = chip_at(*chips[i])
        return pltpu.make_async_remote_copy(
            src_ref=total.at[piece_of(chip), :], dst_ref=total.at[piece_of(chip), :],
            send_sem=send_g.at[i], recv_sem=recv_g.at[i],
            device_id=(z, to * NC + c), device_id_type=MESH,
        )

    def pass_on(chip_id, i):
        return pltpu.make_async_remote_copy(
            src_ref=total.at[piece_of(chip_id), :], dst_ref=total.at[piece_of(chip_id), :],
            send_sem=send_f.at[i], recv_sem=recv_f.at[i],
            device_id=(z, partner), device_id_type=MESH,
        )

    last = len(chips)
    for i in range(last):
        gather_copy(i).start()
    pass_on(chip, last).start()
    for i in reversed(range(last)):
        oy, ox = chips[i]
        gather_copy(i).wait_recv()
        pass_on(chip_at(NY - oy, NX - ox), i).start()
    for i in range(last + 1):
        pass_on(chip, i).wait()
    sum_ref[...] = total[...]

    for i in range(last):
        gather_copy(i).wait_send()
    for oz in range(1, NZ):
        z_copy(oz).wait_send()


def green_call(coef, basis_idx, basis_w, owner_blocks, data, panel_live):
    depth = coef.shape[0]
    rows = data.shape[0]
    k = basis_idx.shape[1]
    chunks = rows // CHUNK
    peers, chips = NDEV - 1, NCHIP - 1
    vmem = pl.BlockSpec(memory_space=pltpu.VMEM)
    smem = pl.BlockSpec(memory_space=pltpu.SMEM)
    anywhere = pl.BlockSpec(memory_space=pl.ANY)
    dma = pltpu.SemaphoreType.DMA
    f32 = jnp.float32
    return pl.pallas_call(
        green_kernel,
        out_shape=(jax.ShapeDtypeStruct((rows, k), f32), jax.ShapeDtypeStruct((2 * HALF, NB), f32)),
        in_specs=[anywhere, smem, anywhere, anywhere, anywhere, anywhere],
        out_specs=(anywhere, vmem),
        scratch_shapes=[
            pltpu.VMEM((chunks, NDEV, depth, CHUNK), jnp.bfloat16),
            pltpu.VMEM((NDEV * depth, k), jnp.bfloat16),
            pltpu.VMEM((rows, k), f32),
            pltpu.SMEM(owner_blocks.shape, jnp.int32),
            pltpu.VMEM(basis_idx.shape, jnp.int32),
            pltpu.VMEM(basis_w.shape, f32),
            pltpu.VMEM((1, rows), f32),
            pltpu.VMEM((SB, k), f32),
            pltpu.VMEM((2 * HALF, NB), f32),
            pltpu.VMEM((HALF, NB), f32),
            pltpu.VMEM((HALF, NB), f32),
            pltpu.VMEM((chips, PIECE, NB), f32),
            pltpu.VMEM((NZ, PIECE, NB), f32),
            pltpu.VMEM((2 * HALF, NB), f32),
            dma((4,)), dma((chunks, peers)), dma((chunks, peers)), dma((chunks,)), dma((chunks,)),
            dma((NY,)), dma((NY,)), dma((chips,)), dma((chips,)), dma((NZ - 1,)), dma((NZ - 1,)),
            dma((chips,)), dma((chips,)), dma((chips + 1,)), dma((chips + 1,)),
        ],
        name="green",
        compiler_params=pltpu.CompilerParams(collective_id=0, has_side_effects=True, vmem_limit_bytes=56 << 20),
    )(owner_blocks, panel_live, coef, basis_idx, basis_w, data.reshape(1, rows))


def dot_hi(a, b, ca, cb):
    return lax.dot_general(a, b, (((ca,), (cb,)), ((), ())), precision=HI, preferred_element_type=jnp.float32)


def dot_3(a, b, ca, cb):
    a_high, a_low = split(a)
    b_high, b_low = split(b)

    def one(left, right):
        return lax.dot_general(left, right, (((ca,), (cb,)), ((), ())), preferred_element_type=jnp.float32)

    return one(a_high, b_high) + (one(a_low, b_high) + one(a_high, b_low))


def factor_block(d, v):
    n = len(d)
    sub = lax.broadcasted_iota(jnp.int32, (SB, NB), 0)

    def bc(part):
        return jnp.broadcast_to(part, (SB, NB))

    for g0 in range(0, n, STRIP):
        scaled = []
        for g in range(g0, g0 + STRIP):
            j0 = SB * g
            def take(i):
                return [bc(d[i][:, j0 + c:j0 + c + 1]) for c in range(SB)]
            cols = take(g)
            steps = []
            iv = None
            for c in range(0, SB, 2):
                e = c + 1
                first = [bc(cols[x][c:e, :]) for x in range(c, SB)]
                second = [bc(cols[x][e:e + 1, :]) for x in range(e, SB)]
                pa, pb, pc = first[0], first[1], second[0]
                rdet = 1.0 / (pa * pc - pb * pb)
                inva = 1.0 / pa
                ka, kb, kc = pa * rdet, pb * rdet, pc * rdet
                pd0, pd1 = bc(d[g][c:e, :]), bc(d[g][e:e + 1, :])
                pv0, pv1 = bc(v[g][c:e, :]), bc(v[g][e:e + 1, :])
                rest = ((first[x - c], second[x - e], x) for x in range(e + 1, SB))
                step = (c, ka, kb, kc, list(rest), pd0, pd1, pv0, pv1)
                steps.append(step)
                u = cols[c] * kc - cols[e] * kb
                t = cols[e] * ka - cols[c] * kb
                u = jnp.where(sub > e, u, jnp.where(sub == e, pb * inva, 0.0))
                t = jnp.where(sub > e, t, 0.0)
                for f, s, x in step[4]:
                    cols[x] = cols[x] - (u * f + t * s)
                d[g] = d[g] - (u * pd0 + t * pd1)
                v[g] = v[g] - (u * pv0 + t * pv1)
                iv = inva if iv is None else jnp.where(sub == c, inva, iv)
                iv = jnp.where(sub == e, ka, iv)
            scaled.append(d[g] * iv)
            for i in range(g + 1, g0 + STRIP):
                cc = take(i)
                for c, ka, kb, kc, rest, pd0, pd1, pv0, pv1 in steps:
                    e = c + 1
                    u = cc[c] * kc - cc[e] * kb
                    t = cc[e] * ka - cc[c] * kb
                    for f, s, x in rest:
                        cc[x] = cc[x] - (u * f + t * s)
                    d[i] = d[i] - (u * pd0 + t * pd1)
                    v[i] = v[i] - (u * pv0 + t * pv1)
        g1 = g0 + STRIP
        if g1 < n:
            left = jnp.concatenate(scaled, axis=0)[:, SB * g1:]
            right = jnp.concatenate([jnp.concatenate(d[g0:g1], axis=0), jnp.concatenate(v[g0:g1], axis=0)], axis=1)
            mv = dot_hi(left, right, 0, 0)
            for i in range(g1, n):
                o = SB * (i - g1)
                d[i] = d[i] - mv[o:o + SB, :NB]
                v[i] = v[i] - mv[o:o + SB, NB:]
    return d, v


def factor_kernel(rows_total, tile, sum_ref, green_ref, r_ref, z_ref, q_ref, a, w, corner, gbuf, qbuf, bsem, gsem, qsem):
    k = r_ref.shape[0]
    rows = green_ref.shape[0]
    nblk = k // NB
    blocks = upper_blocks(k)

    def block_in(i):
        p, q = blocks[i]
        to = corner if i == 0 else a.at[p * NB:(p + 1) * NB, q * NB:(q + 1) * NB]
        return pltpu.make_async_copy(sum_ref.at[i * NB:(i + 1) * NB, :], to, bsem.at[i])

    for i in range(len(blocks)):
        block_in(i).start()
    get = pltpu.make_async_copy(green_ref, gbuf, gsem)
    get.start()

    def clear_lower():
        for p in range(1, nblk):
            a[p * NB:(p + 1) * NB, :p * NB] = jnp.zeros((NB, p * NB), jnp.float32)

    clear_lower()
    w[...] = jnp.zeros_like(w)
    ri = lax.broadcasted_iota(jnp.int32, (NB, NB), 0)
    ci = lax.broadcasted_iota(jnp.int32, (NB, NB), 1)
    eye = jnp.where(ri == ci, 1.0, 0.0)
    block_in(0).wait()
    head = corner[...]
    rhs = jnp.concatenate([head[RHS_AT + i:RHS_AT + i + 1, :RHS_W] for i in range(k // RHS_W)], axis=1)
    a[:NB, :NB] = jnp.where((ri >= RHS_AT) & (ci < RHS_W), jnp.transpose(head), head)

    def panel(p, carry):
        first = pl.multiple_of(p * NB, NB)
        at = pl.ds(first, NB)
        d = [a[pl.ds(first + SB * i, SB), at] for i in range(NB // SB)]
        v = [eye[SB * i:SB * i + SB] for i in range(NB // SB)]
        d, v = factor_block(d, v)
        dd = jnp.concatenate(d, axis=0)
        scale = lax.rsqrt(jnp.sum(jnp.where(ri == ci, dd, 0.0), axis=1, keepdims=True))
        a[at, at] = jnp.where(ri <= ci, dd * scale, 0.0)
        w[at, at] = jnp.where(ri >= ci, jnp.concatenate(v, axis=0) * scale, 0.0)
        for s in range(nblk):
            @pl.when(p == s)
            def _():
                if s == 0:
                    for i in range(1, len(blocks)):
                        block_in(i).wait()
                lo, hi = s * NB, (s + 1) * NB
                inv = w[lo:hi, lo:hi]
                right = k - hi
                parts = ([a[lo:hi, hi:]] if right else []) + ([w[lo:hi, :lo]] if s else [])
                line = dot_3(inv, jnp.concatenate(parts, axis=1) if len(parts) > 1 else parts[0], 1, 0)
                if s:
                    w[lo:hi, :lo] = line[:, right:]
                if right:
                    u = line[:, :right]
                    a[lo:hi, hi:] = u
                    move = dot_3(u, jnp.concatenate([line, inv], axis=1), 0, 0)
                    a[hi:, hi:] = a[hi:, hi:] - move[:, :right]
                    w[hi:, :hi] = w[hi:, :hi] - move[:, right:]
        return carry

    lax.fori_loop(0, nblk, panel, 0)
    clear_lower()
    r_ref[...] = a[...] * (1.0 / rows_total ** 0.5)
    inv_high, inv_low = split(w[...] * (rows_total ** 0.5))

    def q_out(t):
        at = slice(t * tile, (t + 1) * tile)
        return pltpu.make_async_copy(qbuf.at[at, :], q_ref.at[at, :], qsem.at[t])

    def dot_n(left, right):
        return lax.dot_general(left, right, (((1,), (1,)), ((), ())), preferred_element_type=jnp.float32)

    wide = 2 * NB
    rhs_high, rhs_low = split(jnp.broadcast_to(rhs, (SB, k)))
    z = dot_n(rhs_high, inv_high) + (dot_n(rhs_low, inv_high) + dot_n(rhs_high, inv_low))
    z_ref[...] = z[:1] * (1.0 / rows_total ** 0.5)
    get.wait()
    for t in range(rows // tile):
        at = slice(t * tile, (t + 1) * tile)
        high, low = split(gbuf[at, :])
        for n0 in range(0, k, wide):
            n1 = n0 + wide
            right_high, right_low = inv_high[n0:n1, :n1], inv_low[n0:n1, :n1]
            left_high, left_low = high[:, :n1], low[:, :n1]
            qbuf[at, n0:n1] = dot_n(left_high, right_high) + (dot_n(left_low, right_high) + dot_n(left_high, right_low))
        q_out(t).start()
    for t in range(rows // tile):
        q_out(t).wait()


def factor_call(gram_sum, green, rows_total):
    rows, k = green.shape
    tile = 512
    vmem = pl.BlockSpec(memory_space=pltpu.VMEM)
    anywhere = pl.BlockSpec(memory_space=pl.ANY)
    f32 = jnp.float32
    return pl.pallas_call(
        functools.partial(factor_kernel, rows_total, tile),
        out_shape=(jax.ShapeDtypeStruct((k, k), f32), jax.ShapeDtypeStruct((1, k), f32), jax.ShapeDtypeStruct((rows, k), f32)),
        in_specs=[anywhere, anywhere],
        out_specs=(vmem, vmem, anywhere),
        scratch_shapes=[
            pltpu.VMEM((k, k), f32), pltpu.VMEM((k, k), f32), pltpu.VMEM((NB, NB), f32),
            pltpu.VMEM((rows, k), f32), pltpu.VMEM((rows, k), f32),
            pltpu.SemaphoreType.DMA((len(upper_blocks(k)),)), pltpu.SemaphoreType.DMA, pltpu.SemaphoreType.DMA((rows // tile,)),
        ],
        name="factor",
        compiler_params=pltpu.CompilerParams(vmem_limit_bytes=60 << 20),
    )(gram_sum, green)


def on_device(coef, basis_idx, basis_w, owner_blocks, data, panel_live):
    green, gram_sum = green_call(coef, basis_idx, basis_w, owner_blocks, data, panel_live)
    rows_total = green.shape[0] * lax.axis_size("dev") * lax.axis_size("grp")
    r_factor, projected, q_rows = factor_call(gram_sum, green, rows_total)
    return (r_factor, projected.reshape(-1), q_rows)


def solution(mesh):
    in_specs = (P("dev", "grp"), P(), P(), P(), P(("grp", "dev")), P(("grp", "dev")))
    out_specs = (P(), P(), P(("grp", "dev"), None))
    return jax.shard_map(
        on_device, mesh=mesh, in_specs=in_specs, out_specs=out_specs, check_vma=False
    )
```
